32 devices in a mesh: vox: 32 (over z, y, x, core).
Axes of the slice: x: 2, y: 2, z: 4, core: 2. Of those that a mesh axis runs over, the one named last changes fastest.
Arguments:
- voxels: bfloat16 [32768, 512], P('vox'), may hold values from -6 to 6
- hilbert_rank: int32 [32768], P('vox'), may hold values from 0 to 32767, as said below
- z_rank: int32 [32768], P('vox'), may hold values from 0 to 32767, as said below
- parent_slot: int32 [4096], P('vox'), may hold values from 0 to 4095, as said below
- qkv_weight: bfloat16 [2, 512, 1536], replicated, as said below
- out_weight: bfloat16 [2, 512, 512], replicated, may hold values from -0.25 to 0.25
- up_weight: bfloat16 [2, 512, 2048], replicated, may hold values from -0.25 to 0.25
- down_weight: bfloat16 [2, 2048, 512], replicated, may hold values from -0.125 to 0.125
- norm_gains: float32 [2, 2, 512], replicated, may hold values from 0.25 to 1.75
Outputs:
- pooled: float32 [4096, 512], P('vox')
The draws below stay inside these ranges and needn't reach their ends.
Inputs may be any that keep to these rules, and one draw needn't show every extreme that they name: `hilbert_rank`: A permutation. The 1024 voxels of one device have at most 64 Hilbert positions in any one range of 1024 consecutive positions; such counts take only the values 0, 32 and 64, and 64 is reached. `z_rank`: A permutation. The voxels whose Hilbert positions lie in one range of 1024 consecutive positions have at most 64 z ranks in any one such range; counts take only the values 0, 32 and 64, and 64 is reached. `parent_slot`: A permutation. The 128 parents of one range of consecutive parent numbers have at most 8 slots in any one range of 128 consecutive slots; counts take only the values 0, 4 and 8, and 8 is reached. `qkv_weight`: entries of order 512 ** -0.5 times a factor of at most 7.
All inputs are finite; a program needn't handle non-finite values.
Results may differ from the reference program's by a relative error of at most 0.0085.
Values may be sent and summed in bfloat16 or wider, within the bound.
No kernel may reach another device: no remote copies, remote signals or barrier semaphores. Data moves between devices by JAX's collectives and lax.ppermute only.
A program may use at most 128 MiB of HBM per device.

```python
import jax
import jax.numpy as jnp
from jax import lax

D = 512
HEADS = 8
FFN = 2048
PATCH = 1024
BLOCKS = 2
ROWS_DEV = 1024
GROUPS_DEV = 128
TOTAL = 32768
N_VOX = 32


def route_table(seed_key, per_dev, n_dev):
    per_peer = max(per_dev // n_dev, 1)
    strong = per_dev // (4 * per_peer)
    medium = per_dev // (2 * per_peer)
    peer_ids = jnp.arange(n_dev, dtype=jnp.int32)
    seg_sizes = jnp.where(peer_ids < strong, 2 * per_peer, jnp.where(peer_ids < strong + medium, per_peer, 0)).astype(jnp.int32)
    seg_ends = jnp.cumsum(seg_sizes).astype(jnp.int32)
    subkeys = jax.random.split(seed_key, 4)
    source_perm = jax.random.permutation(subkeys[0], n_dev).astype(jnp.int32)
    target_perm = jax.random.permutation(subkeys[1], n_dev).astype(jnp.int32)
    local_slot = jax.vmap(lambda subkey: jax.random.permutation(subkey, per_dev))(jax.random.split(subkeys[2], n_dev)).astype(jnp.int32)
    inner_perm = jax.vmap(lambda subkey: jax.random.permutation(subkey, per_dev))(jax.random.split(subkeys[3], n_dev)).astype(jnp.int32)
    segment = jnp.searchsorted(seg_ends, local_slot, side='right').astype(jnp.int32)
    target_dev = target_perm[(source_perm[:, None] + segment) % n_dev]
    placed = inner_perm[target_dev, local_slot]
    return (target_dev * per_dev + placed).reshape(-1).astype(jnp.int32)


def draw_hilbert_rank(key, part):
    return route_table(jax.random.fold_in(key, 11), ROWS_DEV, N_VOX)


def draw_z_rank(key, part):
    first_map = route_table(jax.random.fold_in(key, 11), ROWS_DEV, N_VOX)
    second_map = route_table(jax.random.fold_in(key, 23), ROWS_DEV, N_VOX)
    return second_map[first_map]


def draw_parent_slot(key, part):
    return route_table(jax.random.fold_in(key, 37), GROUPS_DEV, N_VOX)


def draw_qkv_weight(key, part):
    subkeys = jax.random.split(key, 1)
    drawn_draw = jnp.clip(jax.random.normal(subkeys[0], (BLOCKS, D, 3 * D), jnp.float32), -5.0, 5.0) * D ** (-0.5)
    return drawn_draw.astype(jnp.bfloat16)


def block_scale(own_key, shape, cuts, low, largest):
    level, own = 1.0, jax.random.fold_in(own_key, 6)
    for axis_at, shards_of in cuts:
        steps = jnp.exp(jax.random.uniform(jax.random.fold_in(own, axis_at), (shards_of,), jnp.float32, low / len(cuts), largest / len(cuts)))
        level = level * jnp.repeat(steps, shape[axis_at] // shards_of).reshape([-1 if axis == axis_at else 1 for axis in range(len(shape))])
    return level


def bell_draw(stream_key, shape, spread, most, cuts=(), held_as=jnp.bfloat16):
    drawn = spread * jax.random.normal(stream_key, shape, jnp.float32)
    if cuts:
        drawn = drawn * block_scale(stream_key, shape, cuts, -0.22, 0.18)
    return jnp.clip(drawn, -most, most).astype(held_as)


def setup_inputs(seed: int = 0) -> dict:
    streams_of = jax.random.split(jax.random.key(seed), 10)
    return {
        "voxels": bell_draw(streams_of[0], (TOTAL, D), 1.0, 6.0, ((0, 32),)),
        "hilbert_rank": draw_hilbert_rank(jax.random.fold_in(streams_of[9], 71), 0),
        "z_rank": draw_z_rank(jax.random.fold_in(streams_of[9], 71), 0),
        "parent_slot": draw_parent_slot(jax.random.fold_in(streams_of[9], 71), 0),
        "qkv_weight": draw_qkv_weight(jax.random.fold_in(streams_of[9], 71), 0),
        "out_weight": bell_draw(streams_of[5], (BLOCKS, D, D), D ** -0.5, 0.25),
        "up_weight": bell_draw(streams_of[6], (BLOCKS, D, FFN), D ** -0.5, 0.25),
        "down_weight": bell_draw(streams_of[7], (BLOCKS, FFN, D), FFN ** -0.5, 0.125),
        "norm_gains": jnp.clip(1.0 + 0.15 * jax.random.normal(streams_of[8], (BLOCKS, 2, D), jnp.float32), 0.25, 1.75),
    }


def layer_norm(stream, gain_row):
    row_mean = lax.optimization_barrier(jnp.mean(stream, axis=-1, keepdims=True))
    centred = stream - row_mean
    row_var = lax.optimization_barrier(jnp.mean(centred * centred, axis=-1, keepdims=True))
    return centred * lax.rsqrt(row_var + 1e-05) * gain_row

def patch_block(patch, qkv_w, out_w, up_w, down_w, gain_pair):
    patch_len, feat_width = patch.shape
    head_dim = feat_width // HEADS
    stream = patch.astype(jnp.float32)
    normed = layer_norm(stream, gain_pair[0]).astype(jnp.bfloat16)
    projected = jnp.dot(normed, qkv_w, preferred_element_type=jnp.float32).astype(jnp.bfloat16)
    queries = projected[:, :feat_width].reshape(patch_len, HEADS, head_dim).astype(jnp.float32)
    key_rows = projected[:, feat_width:2 * feat_width].reshape(patch_len, HEADS, head_dim).astype(jnp.float32)
    value_rows = projected[:, 2 * feat_width:].reshape(patch_len, HEADS, head_dim).astype(jnp.float32)
    scores = jnp.einsum('phd,qhd->hpq', queries, key_rows) * head_dim ** (-0.5)
    attn_probs = jax.nn.softmax(scores, axis=-1).astype(jnp.bfloat16)
    attended = jnp.einsum('hpq,qhd->phd', attn_probs.astype(jnp.float32), value_rows)
    attended = attended.reshape(patch_len, feat_width).astype(jnp.bfloat16)
    stream = stream + jnp.dot(attended, out_w, preferred_element_type=jnp.float32)
    normed = layer_norm(stream, gain_pair[1]).astype(jnp.bfloat16)
    inner_act = jax.nn.gelu(jnp.dot(normed, up_w, preferred_element_type=jnp.float32)).astype(jnp.bfloat16)
    return (stream + jnp.dot(inner_act, down_w, preferred_element_type=jnp.float32)).astype(jnp.bfloat16)

def run_block(row_data, qkv_w, out_w, up_w, down_w, gain_pair):
    patches = row_data.reshape(-1, PATCH, row_data.shape[1])
    mapped = lax.map(lambda patch: patch_block(patch, qkv_w, out_w, up_w, down_w, gain_pair), patches)
    return mapped.reshape(row_data.shape)

def reference(voxels, hilbert_rank, z_rank, parent_slot, qkv_weight, out_weight, up_weight, down_weight, norm_gains):
    row_total, feat_width = voxels.shape
    hilbert_rows = jnp.zeros_like(voxels).at[hilbert_rank].set(voxels)
    zpos = jnp.zeros((row_total,), jnp.int32).at[hilbert_rank].set(z_rank)
    first = run_block(hilbert_rows, qkv_weight[0], out_weight[0], up_weight[0], down_weight[0], norm_gains[0])
    z_rows = jnp.zeros_like(first).at[zpos].set(first)
    second = run_block(z_rows, qkv_weight[1], out_weight[1], up_weight[1], down_weight[1], norm_gains[1])
    group_sum = lax.optimization_barrier(jnp.sum(second.reshape(row_total // 8, 8, feat_width).astype(jnp.float32), axis=1))
    pooled = jnp.zeros((row_total // 8, feat_width), jnp.float32).at[parent_slot].set(group_sum)
    return pooled
```

```python
import functools

import jax
import jax.numpy as jnp
from jax import lax
from jax.experimental import pallas as pl
from jax.experimental.pallas import tpu as pltpu
from jax.sharding import PartitionSpec as P

HEADS = 8
LANES = 128
SUB = 8
GROUP = 8
TILE = 256
F32 = jnp.float32
BF16 = jnp.bfloat16
LOG2E = 1.4426950408889634
NT = (((1,), (1,)), ((), ()))


def dot(a, b, dims=(((1,), (0,)), ((), ()))):
    return lax.dot_general(a, b, dims, preferred_element_type=F32)


def iota(shape, axis):
    return lax.broadcasted_iota(jnp.int32, shape, axis)


def log2(value):
    bits = value.bit_length() - 1
    assert 1 << bits == value
    return bits


def rank_rows(dest, n_dev):
    tri = (iota((LANES, LANES), 0) <= iota((LANES, LANES), 1)).astype(F32)
    tri = jnp.concatenate([tri, jnp.ones((LANES, LANES), F32)], axis=1).astype(BF16)
    dev = iota((n_dev, LANES), 0)
    seen = jnp.zeros((n_dev, LANES), F32)
    chunks = []
    for at in range(0, dest.shape[1], LANES):
        hot = (dest[:, at : at + LANES] == dev).astype(F32)
        both = dot(hot.astype(BF16), tri)
        chunks.append((hot, both[:, :LANES] + seen))
        seen = seen + both[:, LANES:]
    return chunks, seen


def starts_of(counts):
    n_dev = counts.shape[0]
    below = (iota((n_dev, n_dev), 1) < iota((n_dev, n_dev), 0)).astype(F32).astype(BF16)
    return dot(below, counts.astype(BF16))


def emit_slots(me, slot_row, meta, rows_of, out_ref, cap, chunks):
    n_dev = out_ref.shape[0]
    per_tile = LANES // cap
    tile = max(TILE, LANES)
    dests = tile // cap
    mine = lax.rem(me, per_tile)
    lane_owner = iota((SUB, LANES), 1) // cap

    def step(t, carry):
        base = t * tile
        hot = (slot_row - base == iota((tile, slot_row.shape[1]), 0)).astype(F32).astype(BF16)
        rows = dot(hot, rows_of()).astype(BF16)
        ids = dot(meta, hot, NT)
        for d in range(dests):
            dev = t * dests + d
            for c in range(chunks):
                out_ref[dev, c * cap : (c + 1) * cap, :] = rows[
                    d * cap : (d + 1) * cap, c * LANES : (c + 1) * LANES
                ]
            part = ids[:, (d // per_tile) * LANES : (d // per_tile + 1) * LANES]
            turn = lax.rem(mine - d % per_tile + per_tile, per_tile) * cap
            part = pltpu.roll(part, turn, 1)
            out_ref[dev, chunks * cap :, :] = jnp.where(lane_owner == mine, part, 0.0).astype(BF16)
        return carry

    lax.fori_loop(0, n_dev // dests, step, 0)


def meta_lanes(got_ref, cap, chunks):
    n_dev = got_ref.shape[0]
    per_tile = LANES // cap
    tiles = []
    for t in range(n_dev // per_tile):
        total = jnp.zeros((SUB, LANES), F32)
        for j in range(per_tile):
            total = total + got_ref[t * per_tile + j, chunks * cap :, :].astype(F32)
        tiles.append(total)
    return jnp.concatenate(tiles, axis=1)


def gather_rows(pos, got_ref, x_ref, cap, chunks, after=None):
    n_dev = got_ref.shape[0]

    def step(t, carry):
        hot = (pos - t * TILE == iota((TILE, pos.shape[1]), 0)).astype(F32).astype(BF16)
        at = pl.ds(pl.multiple_of(t * TILE, TILE), TILE)
        for c in range(0, chunks, 2):
            width = min(2, chunks - c)
            data = jnp.concatenate(
                [
                    got_ref[:, (c + j) * cap : (c + j + 1) * cap, :].reshape(n_dev * cap, LANES)
                    for j in range(width)
                ],
                axis=1,
            )
            x_ref[at, c * LANES : (c + width) * LANES] = dot(hot, data)
        if after is not None:
            after(t, hot)
        return carry

    lax.fori_loop(0, x_ref.shape[0] // TILE, step, 0)


def layer_norm(stream, gain_row):
    row_mean = jnp.mean(stream, axis=-1, keepdims=True)
    centred = stream - row_mean
    row_var = jnp.mean(centred * centred, axis=-1, keepdims=True)
    return centred * lax.rsqrt(row_var + 1e-05) * gain_row


def block_tiles(x_ref, qkv_ref, att_ref, weights, gains, finish):
    qkv_w, out_w, up_w, down_w = weights
    rows, width = x_ref.shape
    head = width // HEADS
    pairs = width // LANES
    per_pair = LANES // head
    tiles = rows // TILE

    def project(t, carry):
        at = pl.ds(pl.multiple_of(t * TILE, TILE), TILE)
        normed = layer_norm(x_ref[at, :], gains[0:1, :]).astype(BF16)
        for c, scale in ((0, LOG2E * head**-0.5), (1, None), (2, None)):
            part = dot(normed, qkv_w[:, c * width : (c + 1) * width])
            if scale is not None:
                part = part * scale
            qkv_ref[at, c * width : (c + 1) * width] = part.astype(BF16)
        return carry

    lax.fori_loop(0, tiles, project, 0)
    ones = jnp.ones((rows, LANES), BF16)
    owner = iota((TILE, LANES), 1) // head

    def attend(t, carry):
        at = pl.ds(pl.multiple_of(t * TILE, TILE), TILE)
        for pair in range(pairs):
            cols = slice(pair * LANES, (pair + 1) * LANES)
            queries = qkv_ref[at, cols]
            key_rows = qkv_ref[:, width + pair * LANES : width + (pair + 1) * LANES]
            value_rows = qkv_ref[:, 2 * width + pair * LANES : 2 * width + (pair + 1) * LANES]
            value_rows = jnp.concatenate([value_rows, ones], axis=1)
            merged = None
            for h in range(per_pair):
                own = jnp.where(owner == h, queries, jnp.zeros_like(queries))
                scores = dot(own, key_rows, NT)
                top = jnp.max(scores, axis=1, keepdims=True)
                probs = jnp.exp2(scores - top).astype(BF16)
                mixed = dot(probs, value_rows)
                mixed = mixed[:, :LANES] / mixed[:, LANES:]
                merged = mixed if merged is None else jnp.where(owner == h, mixed, merged)
            att_ref[:, cols] = merged.astype(BF16)
        stream = x_ref[at, :] + dot(att_ref[...], out_w[...])
        normed = layer_norm(stream, gains[1:2, :]).astype(BF16)
        inner = jax.nn.gelu(dot(normed, up_w[...])).astype(BF16)
        finish(t, stream + dot(inner, down_w[...]))
        return carry

    lax.fori_loop(0, tiles, attend, 0)


def load_weights(block, hbm, vmem, sems):
    copies = [
        pltpu.make_async_copy(src.at[block], dst, sems.at[i])
        for i, (src, dst) in enumerate(zip(hbm, vmem))
    ]
    for copy in copies:
        copy.start()
    return copies


def pack_kernel(me_ref, hil_ref, z_ref, x_ref, out_ref, *, cap):
    rows, width = x_ref.shape
    n_dev = out_ref.shape[0]
    shift = log2(rows)
    z = z_ref[...]
    z_low = z & (rows - 1)
    meta = jnp.concatenate([(z >> shift) + 1, z_low >> 3, z_low & 7, jnp.zeros((SUB - 3, rows), jnp.int32)], axis=0)
    dest = hil_ref[...] >> shift
    chunks, _ = rank_rows(dest, n_dev)
    dev = iota((n_dev, LANES), 0).astype(F32) * cap
    slot = jnp.concatenate(
        [jnp.sum(hot * (run - 1 + dev), axis=0, keepdims=True) for hot, run in chunks], axis=1
    ).astype(jnp.int32)
    emit_slots(me_ref[0], slot, meta.astype(F32).astype(BF16), lambda: x_ref[...], out_ref, cap, width // LANES)


def first_kernel(
    me_ref, got_ref, gains_ref, qkv_hbm, out_hbm, up_hbm, down_hbm, send_ref,
    x_ref, y_ref, ids_ref, qkv_ref, att_ref, qkv_w, out_w, up_w, down_w, sems, *, cap
):
    rows, width = x_ref.shape
    n_dev = got_ref.shape[0]
    lanes_of = width // LANES
    weights = (qkv_w, out_w, up_w, down_w)
    copies = load_weights(0, (qkv_hbm, out_hbm, up_hbm, down_hbm), weights, sems)
    ids = meta_lanes(got_ref, cap, lanes_of)
    dest = ids[0:1, :].astype(jnp.int32) - 1
    chunks, counts = rank_rows(dest, n_dev)
    starts = starts_of(counts)
    pos = jnp.concatenate(
        [
            jnp.sum(hot * (run + starts), axis=0, keepdims=True) - 1
            for hot, run in chunks
        ],
        axis=1,
    ).astype(jnp.int32)
    ids16 = ids.astype(BF16)

    def keep_ids(t, hot):
        ids_ref[:, pl.ds(pl.multiple_of(t * TILE, TILE), TILE)] = dot(ids16, hot, NT)

    gather_rows(pos, got_ref, x_ref, cap, lanes_of, keep_ids)
    for copy in copies:
        copy.wait()

    def finish(t, value):
        y_ref[pl.ds(pl.multiple_of(t * TILE, TILE), TILE), :] = value.astype(BF16)

    block_tiles(x_ref, qkv_ref, att_ref, weights, gains_ref[0], finish)
    slots = []
    dev = iota((n_dev, LANES), 0).astype(F32) * cap
    for at in range(0, rows, LANES):
        k = (iota((n_dev, LANES), 1) + at).astype(F32)
        inside = ((k >= starts) & (k < starts + counts)).astype(F32)
        slots.append(jnp.sum(inside * (dev + k - starts), axis=0, keepdims=True))
    slot = jnp.concatenate(slots, axis=1).astype(jnp.int32)
    emit_slots(me_ref[0], slot, ids_ref[...].astype(BF16), lambda: y_ref[...], send_ref, cap, lanes_of)


def second_kernel(
    got_ref, gains_ref, child_ref, label_ref, qkv_hbm, out_hbm, up_hbm, down_hbm, send_ref,
    x_ref, y_ref, qkv_ref, att_ref, qkv_w, out_w, up_w, down_w, sems, *, cap, cap_groups
):
    rows, width = x_ref.shape
    n_dev = got_ref.shape[0]
    lanes_of = width // LANES
    weights = (qkv_w, out_w, up_w, down_w)
    copies = load_weights(1, (qkv_hbm, out_hbm, up_hbm, down_hbm), weights, sems)
    ids = meta_lanes(got_ref, cap, lanes_of).astype(jnp.int32)
    pos = jnp.where(ids[0:1, :] > 0, ids[1:2, :] * GROUP + ids[2:3, :], -1)
    gather_rows(pos, got_ref, x_ref, cap, lanes_of)
    for copy in copies:
        copy.wait()

    def finish(t, value):
        y_ref[pl.ds(pl.multiple_of(t * TILE, TILE), TILE), :] = value.astype(BF16)

    block_tiles(x_ref, qkv_ref, att_ref, weights, gains_ref[1], finish)
    dest = child_ref[...] >> log2(rows // GROUP)
    chunks, _ = rank_rows(dest, n_dev)
    dev = iota((n_dev, LANES), 0).astype(F32) * (cap_groups * GROUP)
    slot = jnp.concatenate(
        [jnp.sum(hot * (run - 1 + dev), axis=0, keepdims=True) for hot, run in chunks], axis=1
    ).astype(jnp.int32) >> 3
    hot = (slot == iota((n_dev * cap_groups, rows), 0)).astype(F32).astype(BF16)
    send_ref[:, :width] = dot(hot, y_ref[...]).astype(BF16)
    send_ref[:, width:] = (dot(hot, label_ref[...]) * (1.0 / GROUP)).astype(BF16)


def pool_kernel(got_ref, out_ref):
    groups, width = out_ref.shape
    slots = got_ref.shape[0]
    label = got_ref[:, width:].astype(jnp.int32) - 1
    hot = (label == iota((slots, groups), 1)).astype(F32).astype(BF16)
    out_ref[...] = dot(hot, got_ref[:, :width], (((0,), (0,)), ((), ())))


VMEM = pl.BlockSpec(memory_space=pltpu.VMEM)
SMEM = pl.BlockSpec(memory_space=pltpu.SMEM)
ANY = pl.BlockSpec(memory_space=pl.ANY)
PARAMS = pltpu.CompilerParams(vmem_limit_bytes=56 * 1024 * 1024)


def exchange(data):
    return lax.all_to_all(data, "vox", split_axis=0, concat_axis=0, tiled=True)


def shards(
    voxels, hilbert_rank, z_rank, parent_slot, qkv_weight, out_weight, up_weight, down_weight, norm_gains
):
    rows, width = voxels.shape
    n_dev = lax.axis_size("vox")
    me = lax.axis_index("vox").astype(jnp.int32).reshape(1)
    cap = 2 * max(rows // n_dev, 1)
    groups = rows // GROUP
    cap_groups = 2 * max(groups // n_dev, 1)
    slot_rows = width // LANES * cap + SUB
    slots = jax.ShapeDtypeStruct((n_dev, slot_rows, LANES), BF16)
    weights = (qkv_weight, out_weight, up_weight, down_weight)
    weight_scratch = [pltpu.VMEM(w.shape[1:], BF16) for w in weights] + [pltpu.SemaphoreType.DMA((4,))]
    work = [pltpu.VMEM((rows, 3 * width), BF16), pltpu.VMEM((TILE, width), BF16)]

    child = jnp.repeat(parent_slot, GROUP)
    label = jnp.broadcast_to(((child & (groups - 1)) + 1)[:, None], (rows, LANES)).astype(BF16)

    send = pl.pallas_call(
        functools.partial(pack_kernel, cap=cap),
        out_shape=slots,
        in_specs=[SMEM, VMEM, VMEM, VMEM],
        out_specs=VMEM,
        compiler_params=PARAMS,
        name="pack",
    )(me, hilbert_rank.reshape(1, rows), z_rank.reshape(1, rows), voxels)
    got = exchange(send)
    send = pl.pallas_call(
        functools.partial(first_kernel, cap=cap),
        out_shape=slots,
        in_specs=[SMEM, VMEM, VMEM, ANY, ANY, ANY, ANY],
        out_specs=VMEM,
        scratch_shapes=[
            pltpu.VMEM((rows, width), F32),
            pltpu.VMEM((rows, width), BF16),
            pltpu.VMEM((SUB, rows), F32),
            *work,
            *weight_scratch,
        ],
        compiler_params=PARAMS,
        name="first",
    )(me, got, norm_gains, *weights)
    got = exchange(send)
    send = pl.pallas_call(
        functools.partial(second_kernel, cap=cap, cap_groups=cap_groups),
        out_shape=jax.ShapeDtypeStruct((n_dev * cap_groups, width + LANES), BF16),
        in_specs=[VMEM, VMEM, VMEM, VMEM, ANY, ANY, ANY, ANY],
        out_specs=VMEM,
        scratch_shapes=[
            pltpu.VMEM((rows, width), F32),
            pltpu.VMEM((rows, width), BF16),
            *work,
            *weight_scratch,
        ],
        compiler_params=PARAMS,
        name="second",
    )(got, norm_gains, child.reshape(1, rows), label, *weights)
    got = exchange(send.reshape(n_dev, cap_groups, width + LANES))
    return pl.pallas_call(
        pool_kernel,
        out_shape=jax.ShapeDtypeStruct((groups, width), F32),
        in_specs=[VMEM],
        out_specs=VMEM,
        compiler_params=PARAMS,
        name="pool",
    )(got.reshape(n_dev * cap_groups, width + LANES))


def solution(mesh):
    placed = (P("vox", None), P("vox"), P("vox"), P("vox"), P(), P(), P(), P(), P())
    return jax.shard_map(
        shards, mesh=mesh, in_specs=placed, out_specs=P("vox", None), check_vma=False
    )
```

```python
import functools

import jax
import jax.numpy as jnp
from jax import lax
from jax.experimental import pallas as pl
from jax.experimental.pallas import tpu as pltpu
from jax.sharding import PartitionSpec as P

HEADS = 8
LANES = 128
SUB = 8
GROUP = 8
TILE = 256
PART = 16
LABEL_ROW = 7
F32 = jnp.float32
BF16 = jnp.bfloat16
I32 = jnp.int32
LOG2E = 1.4426950408889634
GELU_C = 0.7978845608028654
ONES = 16
NT = (((1,), (1,)), ((), ()))


def dot(a, b, dims=(((1,), (0,)), ((), ()))):
    return lax.dot_general(a, b, dims, preferred_element_type=F32)


def iota(shape, axis):
    return lax.broadcasted_iota(I32, shape, axis)


def one_hot(mask):
    return mask.astype(F32).astype(BF16)


def log2(value):
    bits = value.bit_length() - 1
    assert 1 << bits == value
    return bits


def tile_at(t):
    return pl.ds(t * TILE if isinstance(t, int) else pl.multiple_of(t * TILE, TILE), TILE)


def lane_cuts(size):
    return range(0, size, LANES)


def rank_rows(dest, n_dev):
    tri = (iota((LANES, LANES), 0) <= iota((LANES, LANES), 1)).astype(F32)
    tri = jnp.concatenate([tri, jnp.ones((LANES, LANES), F32)], axis=1).astype(BF16)
    dev = iota((n_dev, LANES), 0)
    seen = jnp.zeros((n_dev, LANES), F32)
    chunks = []
    for at in lane_cuts(dest.shape[1]):
        hot = (dest[:, at : at + LANES] == dev).astype(F32)
        both = dot(hot.astype(BF16), tri)
        chunks.append((hot, both[:, :LANES] + seen))
        seen = seen + both[:, LANES:]
    return chunks, seen


def pick(hot, table):
    return jnp.sum(hot * table, axis=0, keepdims=True)


def part_starts(counts, parts):
    n_dev = counts.shape[0]
    below = one_hot(iota((n_dev, n_dev), 1) < iota((n_dev, n_dev), 0))
    return dot(below, counts.astype(BF16)) * (1.0 / parts)


def sort_places(dest, n_dev, rows, parts):
    chunks, counts = rank_rows(dest, n_dev)
    starts = part_starts(counts, parts)
    part_rows = rows // parts
    cap = parts * PART
    places = []
    for hot, run in chunks:
        order = pick(hot, run - 1).astype(I32)
        count = pick(hot, counts).astype(I32)
        start = pick(hot, starts).astype(I32)
        full = count == cap
        part = jnp.where(full, order >> log2(PART), order >> log2(PART // 2))
        inside = order - part * jnp.where(full, PART, PART // 2)
        places.append(jnp.where(count > 0, part * part_rows + start + inside, -1))
    return jnp.concatenate(places, axis=1), counts, starts


def part_slots(counts, starts, part_rows, parts):
    n_dev = counts.shape[0]
    share = counts * (1.0 / parts)
    dev = iota((n_dev, LANES), 0).astype(F32) * PART
    slots = []
    for at in lane_cuts(part_rows):
        k = (iota((n_dev, LANES), 1) + at).astype(F32)
        inside = ((k >= starts) & (k < starts + share)).astype(F32)
        slots.append(pick(inside, dev + k - starts))
    return jnp.concatenate(slots, axis=1).astype(I32)


def group_slots(parent, n_dev, stride):
    chunks, _ = rank_rows(parent >> log2(parent.shape[1]), n_dev)
    dev = iota((n_dev, LANES), 0).astype(F32) * stride
    return jnp.concatenate([pick(hot, run - 1 + dev) for hot, run in chunks], axis=1).astype(I32)


def emit_rows(slot_row, rows, meta, group, out_ref, ids_ref):
    span = (out_ref.shape[1] - SUB) // (rows.shape[1] // LANES)
    for t in range(ids_ref.shape[1] // TILE):
        hot = one_hot(slot_row - t * TILE == iota((TILE, slot_row.shape[1]), 0))
        placed = dot(hot, rows).astype(BF16)
        ids_ref[:, tile_at(t)] += dot(meta, hot, NT)
        for d in range(TILE // PART):
            for c in range(rows.shape[1] // LANES):
                at = c * span + group * PART
                out_ref[t * (TILE // PART) + d, at : at + PART, :] = placed[
                    d * PART : (d + 1) * PART, c * LANES : (c + 1) * LANES
                ]


def emit_ids(me, out_ref, ids_ref):
    per_tile = LANES // PART
    mine = lax.rem(me, per_tile)
    owned = iota((SUB, LANES), 1) // PART == mine
    at = out_ref.shape[1] - SUB
    for dev in range(out_ref.shape[0]):
        cut = dev // per_tile * LANES
        turn = lax.rem(mine + (per_tile - dev % per_tile), per_tile) * PART
        part = pltpu.roll(ids_ref[:, cut : cut + LANES], turn, 1)
        out_ref[dev, at:, :] = jnp.where(owned, part, 0.0).astype(BF16)


def slot_ids(got_ref):
    n_dev, depth, _ = got_ref.shape
    per_tile = LANES // PART
    tiles = []
    for first in range(0, n_dev, per_tile):
        total = got_ref[first, depth - SUB :, :].astype(F32)
        for j in range(1, per_tile):
            total = total + got_ref[first + j, depth - SUB :, :].astype(F32)
        tiles.append(total)
    return jnp.concatenate(tiles, axis=1)


def slot_rows(got_ref, group, lanes_of):
    n_dev, depth, _ = got_ref.shape
    span = (depth - SUB) // lanes_of
    return jnp.concatenate(
        [
            got_ref[:, c * span + group * PART : c * span + (group + 1) * PART, :].reshape(n_dev * PART, LANES)
            for c in range(lanes_of)
        ],
        axis=1,
    )


def layer_norm(stream, gain_row):
    row_mean = jnp.mean(stream, axis=-1, keepdims=True)
    centred = stream - row_mean
    row_var = jnp.mean(centred * centred, axis=-1, keepdims=True)
    return centred * lax.rsqrt(row_var + 1e-05) * gain_row


def gelu(x):
    inner = x * (x * x * (0.044715 * GELU_C) + GELU_C)
    half = 0.5 * x
    return half + half * jnp.tanh(inner)


def project_tile(t, x_ref, qk_ref, vt_ref, qkv_w, gains):
    width = x_ref.shape[1]
    head = width // HEADS
    at = tile_at(t)
    normed = layer_norm(x_ref[at, :].astype(F32), gains[0:1, :]).astype(BF16)
    qk_ref[at, :width] = (dot(normed, qkv_w[:, :width]) * (LOG2E * head**-0.5)).astype(BF16)
    qk_ref[at, width:] = dot(normed, qkv_w[:, width : 2 * width]).astype(BF16)
    values = dot(normed, qkv_w[:, 2 * width :]).T.astype(BF16)
    for h in range(HEADS):
        vt_ref[h, :head, at] = values[h * head : (h + 1) * head, :]


def fill_ones(vt_ref):
    depth = vt_ref.shape[1]
    for h in range(HEADS):
        vt_ref[h, depth - ONES :, :] = jnp.ones((ONES, vt_ref.shape[2]), BF16)


def run_tiles(low, high, x_ref, y_ref, state, weights, gains):
    qk_ref, vt_ref, att_ref, mid_ref, sum_ref, score_ref = state
    _, out_w, up_w, down_w = weights
    rows, width = x_ref.shape
    head = width // HEADS
    pairs = width // LANES
    per_pair = LANES // head
    piece = up_w.shape[1] // pairs
    owner = iota((TILE, LANES), 1) // head
    cuts = [slice(at, at + TILE) for at in range(0, rows, TILE)]

    def masked_queries(t, pair):
        queries = qk_ref[tile_at(t), pair * LANES : (pair + 1) * LANES]
        return [jnp.where(owner == j, queries, jnp.zeros_like(queries)) for j in range(per_pair)]

    def score_cut(own, pair, cut, tops):
        key_rows = qk_ref[cut, width + pair * LANES : width + (pair + 1) * LANES]
        result = []
        for j in range(per_pair):
            scores = dot(key_rows, own[j], NT)
            score_ref[pair % 2, j, cut, :] = scores
            top = jnp.max(scores.reshape(TILE // SUB, SUB, TILE), axis=0)
            result.append(top if tops is None else jnp.maximum(tops[j], top))
        return result

    def mix_cut(pair, cut, tops, sums):
        result = []
        for j in range(per_pair):
            probs = jnp.exp2(score_ref[pair % 2, j, cut, :] - tops[j]).astype(BF16)
            mixed = dot(vt_ref[pair * per_pair + j, :, cut], probs)
            result.append(mixed if sums is None else sums[j] + mixed)
        return result

    def attend_pair(pair, tops, next_tile):
        after = (pair + 1) % pairs
        own = None if next_tile is None else masked_queries(next_tile, after)
        tops = [jnp.max(top, axis=0, keepdims=True) for top in tops]
        next_tops, sums = None, None
        for cut in cuts:
            if own is not None:
                next_tops = score_cut(own, after, cut, next_tops)
            sums = mix_cut(pair, cut, tops, sums)
        for j in range(per_pair):
            h = pair * per_pair + j
            share = 1.0 / sums[j][head : head + SUB, :]
            mixed = sums[j][:head, :].reshape(head // SUB, SUB, TILE) * share[None]
            att_ref[h * head : (h + 1) * head, :] = mixed.reshape(head, TILE)
        return next_tops

    def join(t):
        attended = att_ref[...].T.astype(BF16)
        stream = x_ref[tile_at(t), :].astype(F32) + dot(attended, out_w[...])
        sum_ref[...] = stream
        mid_ref[...] = layer_norm(stream, gains[1:2, :]).astype(BF16)

    def mlp_piece(i):
        cut = slice(i * piece, (i + 1) * piece)
        inner = gelu(dot(mid_ref[...], up_w[:, cut])).astype(BF16)
        sum_ref[...] += dot(inner, down_w[cut, :])

    def attend_tile(t, tops, after, beside):
        for i in range(pairs):
            tops = attend_pair(i, tops, t if i + 1 < pairs else after)
            if beside:
                mlp_piece(i)
        return tops

    def step(t, tops):
        join(t - 1)
        tops = attend_tile(t, tops, jnp.minimum(t + 1, high - 1), True)
        y_ref[tile_at(t - 1), :] = sum_ref[...].astype(BF16)
        return tops

    own = masked_queries(low, 0)
    tops = None
    for cut in cuts:
        tops = score_cut(own, 0, cut, tops)
    tops = attend_tile(low, tops, low + 1 if high > low + 1 else None, False)
    if high > low + 1:
        lax.fori_loop(low + 1, high, step, tops)
    join(high - 1)
    for i in range(pairs):
        mlp_piece(i)
    y_ref[tile_at(high - 1), :] = sum_ref[...].astype(BF16)


def start_loads(block, hbm, vmem, sems):
    copies = [
        pltpu.make_async_copy(src.at[block], dst, sems.at[i])
        for i, (src, dst) in enumerate(zip(hbm, vmem))
    ]
    for copy in copies:
        copy.start()
    return copies


def pack_kernel(me_ref, hil_ref, z_ref, x_ref, out_ref, ids_ref, *, parts):
    rows, width = x_ref.shape
    n_dev = out_ref.shape[0]
    part_rows = rows // parts
    shift = log2(rows)
    z = z_ref[...]
    pair = jnp.concatenate([(z >> shift) + 1, (z & (rows - 1)) >> log2(GROUP)], axis=0)
    meta = jnp.concatenate([pair] * (SUB // 2), axis=0).astype(F32).astype(BF16)
    places, counts, starts = sort_places(hil_ref[...] >> shift, n_dev, rows, parts)
    slot_row = part_slots(counts, starts, part_rows, parts)
    ids_ref[...] = jnp.zeros_like(ids_ref)
    for q in range(parts):
        hot = one_hot(places - q * part_rows == iota((part_rows, rows), 0))
        sorted_rows = dot(hot, x_ref[...]).astype(BF16)
        ids = dot(meta, hot, NT)
        ids = jnp.where(iota(ids.shape, 0) // 2 == q, ids, 0.0).astype(BF16)
        emit_rows(slot_row, sorted_rows, ids, q, out_ref, ids_ref)
    emit_ids(me_ref[0], out_ref, ids_ref)


def emit_block(me, groups, base, slot_row, y_ref, parents, send_ref, ids_ref):
    part_rows = slot_row.shape[1]
    for g in groups:
        at = slice(g * part_rows, (g + 1) * part_rows)
        meta = parents[:, at]
        meta = jnp.where(iota(meta.shape, 0) == g - base, meta, 0.0).astype(BF16)
        emit_rows(slot_row, y_ref[at, :], meta, g - base, send_ref, ids_ref)
    emit_ids(me, send_ref, ids_ref)


def open_kernel(me_ref, got_ref, parent_ref, gains_ref, *refs, parts, split):
    hbm, refs = refs[:4], refs[4:]
    if split:
        (send_ref, x_out, qk_out, vt_out, ids_out, slot_out), refs = refs[:6], refs[6:]
    else:
        (send_ref,), refs = refs[:1], refs[1:]
    x_ref, y_ref, parents_ref, ids_ref = refs[:4]
    state, weights, sems, out_sems = refs[4:10], refs[10:14], refs[14], refs[15]
    qk_ref, vt_ref = state[:2]
    rows, width = x_ref.shape
    n_dev = got_ref.shape[0]
    part_rows = rows // parts
    lanes_of = width // LANES
    loads = start_loads(0, hbm, weights, sems)
    gains = gains_ref[0]
    fill_ones(vt_ref)

    ids = slot_ids(got_ref)
    dest = jnp.concatenate([ids[2 * g : 2 * g + 1, :] for g in range(parts)], axis=1).astype(I32) - 1
    parents = jnp.concatenate([ids[2 * g + 1 : 2 * g + 2, :] for g in range(parts)], axis=1) + 1.0
    parents = jnp.broadcast_to(parents, (SUB, parents.shape[1])).astype(BF16)
    places, counts, starts = sort_places(dest, n_dev, rows, parts)
    slot_row = part_slots(counts, starts, part_rows, parts)

    loads[0].wait()

    def receive(t, carry):
        hot = one_hot(places - t * TILE == iota((TILE, places.shape[1]), 0))
        for c in range(0, lanes_of, 2):
            data = jnp.concatenate([slot_rows_cut(got_ref, g, c, lanes_of) for g in range(parts)], axis=0)
            x_ref[tile_at(t), c * LANES : (c + 2) * LANES] = dot(hot, data).astype(BF16)
        parents_ref[:, tile_at(t)] = dot(parents, hot, NT)
        return carry

    lax.fori_loop(0, rows // TILE, receive, 0)

    def project(t, carry):
        project_tile(t, x_ref, qk_ref, vt_ref, weights[0], gains)
        return carry

    lax.fori_loop(0, rows // TILE, project, 0)
    saves = []
    if split:
        ids_out[...] = parents_ref[...]
        slot_out[...] = jnp.broadcast_to(slot_row, slot_out.shape)
        saves = [
            pltpu.make_async_copy(src, dst, out_sems.at[i])
            for i, (src, dst) in enumerate(((x_ref, x_out), (qk_ref, qk_out), (vt_ref, vt_out)))
        ]
        for save in saves:
            save.start()
    for load in loads[1:]:
        load.wait()
    groups = 1 if split else parts
    run_tiles(0, groups * part_rows // TILE, x_ref, y_ref, state, weights, gains)

    ids_ref[...] = jnp.zeros_like(ids_ref)
    parent = parent_ref[...]
    label_slot = group_slots(parent, n_dev, PART)
    low = (parent & (parent.shape[1] - 1)) + 1
    low = jnp.broadcast_to(low, (SUB, low.shape[1])).astype(F32)
    low = jnp.where(iota(low.shape, 0) == LABEL_ROW, low, 0.0).astype(BF16)
    for t in range(ids_ref.shape[1] // TILE):
        hot = one_hot(label_slot - t * TILE == iota((TILE, label_slot.shape[1]), 0))
        ids_ref[:, tile_at(t)] += dot(low, hot, NT)
    emit_block(me_ref[0], range(groups), 0, slot_row, y_ref, parents_ref[...], send_ref, ids_ref)
    for save in saves:
        save.wait()


def slot_rows_cut(got_ref, group, c, lanes_of):
    n_dev, depth, _ = got_ref.shape
    span = (depth - SUB) // lanes_of
    return jnp.concatenate(
        [
            got_ref[:, j * span + group * PART : j * span + (group + 1) * PART, :].reshape(n_dev * PART, LANES)
            for j in (c, c + 1)
        ],
        axis=1,
    )


def rest_kernel(me_ref, x_ref, qk_ref, vt_ref, parents_ref, slot_ref, gains_ref, *refs, parts):
    hbm, send_ref, y_ref, ids_ref = refs[:4], refs[4], refs[5], refs[6]
    scratch, weights, sems = refs[7:11], refs[11:14], refs[14]
    loads = start_loads(0, hbm[1:], weights, sems)
    for load in loads:
        load.wait()
    rows = x_ref.shape[0]
    run_tiles(
        rows // parts // TILE, rows // TILE, x_ref, y_ref, (qk_ref, vt_ref, *scratch), (None, *weights), gains_ref[0]
    )
    ids_ref[...] = jnp.zeros_like(ids_ref)
    emit_block(me_ref[0], range(1, parts), 1, slot_ref[0:1, :], y_ref, parents_ref[...], send_ref, ids_ref)


def second_kernel(*refs, parts, chunks, cap_groups):
    got_refs, refs = refs[:chunks], refs[chunks:]
    (parent_ref, gains_ref), hbm, (send_ref, label_ref), refs = refs[:2], refs[2:6], refs[6:8], refs[8:]
    x_ref, y_ref, parents_ref = refs[:3]
    state, weights, sems = refs[3:9], refs[9:13], refs[13]
    rows, width = x_ref.shape
    n_dev = got_refs[0].shape[0]
    part_rows = rows // parts
    loads = start_loads(1, hbm, weights, sems)
    gains = gains_ref[1]
    fill_ones(state[1])

    part = 0
    for k, got_ref in enumerate(got_refs):
        ids = slot_ids(got_ref)
        if k == 0:
            slots = n_dev * cap_groups
            wide, slim = iota((n_dev * PART, slots), 0), iota((n_dev * PART, slots), 1)
            order = slim & (cap_groups - 1)
            narrow = one_hot(wide == (slim >> log2(cap_groups)) * PART + order)
            label_ref[...] = dot(ids.astype(BF16), narrow)
        for g in range(parts if chunks == 1 else (1, parts - 1)[k]):
            own = ids[g : g + 1, :]
            ranks, _ = rank_rows(jnp.where(own > 0.0, 0, -1), SUB)
            places = jnp.concatenate([pick(hot, run) for hot, run in ranks], axis=1).astype(I32) - 1
            own = jnp.broadcast_to(own, ids.shape).astype(BF16)
            for t in range(part_rows // TILE):
                hot = one_hot(places - t * TILE == iota((TILE, places.shape[1]), 0))
                at = tile_at(part * (part_rows // TILE) + t)
                x_ref[at, :] = dot(hot, slot_rows(got_ref, g, width // LANES)).astype(BF16)
                parents_ref[:, at] = dot(own, hot, NT)
            part += 1

    loads[0].wait()

    def project(t, carry):
        project_tile(t, x_ref, state[0], state[1], weights[0], gains)
        return carry

    lax.fori_loop(0, rows // TILE, project, 0)
    for load in loads[1:]:
        load.wait()
    run_tiles(0, rows // TILE, x_ref, y_ref, state, weights, gains)

    groups = rows // GROUP
    member = one_hot(parents_ref[0:1, :].astype(I32) - 1 == iota((groups, rows), 0))
    sums = dot(member, y_ref[...]).astype(BF16)
    slot = group_slots(parent_ref[...], n_dev, cap_groups)
    send_ref[...] = dot(one_hot(slot == iota((send_ref.shape[0], groups), 0)), sums).astype(BF16)


def pool_kernel(label_ref, got_ref, out_ref):
    label = label_ref[LABEL_ROW : LABEL_ROW + 1, :].astype(I32) - 1
    hot = one_hot(label == iota((out_ref.shape[0], label.shape[1]), 0))
    out_ref[...] = dot(hot, got_ref[...])


VMEM = pl.BlockSpec(memory_space=pltpu.VMEM)
SMEM = pl.BlockSpec(memory_space=pltpu.SMEM)
ANY = pl.BlockSpec(memory_space=pl.ANY)


def call(body, name, outs, in_specs, out_specs=VMEM, scratch=(), flops=0):
    return pl.pallas_call(
        body,
        out_shape=outs,
        in_specs=in_specs,
        out_specs=out_specs,
        scratch_shapes=list(scratch),
        compiler_params=pltpu.CompilerParams(vmem_limit_bytes=56 * 1024 * 1024),
        cost_estimate=pl.CostEstimate(flops=flops, bytes_accessed=flops // 300, transcendentals=0),
        name=name,
    )


def exchange(data):
    return lax.all_to_all(data, "vox", split_axis=0, concat_axis=0, tiled=True)


def shards(
    voxels, hilbert_rank, z_rank, parent_slot, qkv_weight, out_weight, up_weight, down_weight, norm_gains
):
    rows, width = voxels.shape
    n_dev = lax.axis_size("vox")
    me = lax.axis_index("vox").astype(I32).reshape(1)
    cap = 2 * max(rows // n_dev, 1)
    parts = max(cap // PART, 1)
    groups = rows // GROUP
    cap_groups = 2 * max(groups // n_dev, 1)
    lanes_of = width // LANES
    weights = (qkv_weight, out_weight, up_weight, down_weight)
    weight_scratch = [pltpu.VMEM(w.shape[1:], BF16) for w in weights]
    parent = parent_slot.reshape(1, groups)
    full_flops = 9_000_000 * rows

    def slots(part_count):
        return jax.ShapeDtypeStruct((n_dev, lanes_of * part_count * PART + SUB, LANES), BF16)

    qk = ((rows, 2 * width), BF16)
    vt = ((HEADS, width // HEADS + ONES, rows), BF16)
    tile_scratch = [
        pltpu.VMEM((width, TILE), F32),
        pltpu.VMEM((TILE, width), BF16),
        pltpu.VMEM((TILE, width), F32),
        pltpu.VMEM((2, LANES * HEADS // width, rows, TILE), F32),
    ]
    patch = pltpu.VMEM((rows, width), BF16)
    id_rows = pltpu.VMEM((SUB, rows), F32)
    slot_ids_scratch = pltpu.VMEM((SUB, n_dev * PART), F32)

    send = call(
        functools.partial(pack_kernel, parts=parts),
        "pack",
        slots(parts),
        [SMEM, VMEM, VMEM, VMEM],
        scratch=[slot_ids_scratch],
    )(me, hilbert_rank.reshape(1, rows), z_rank.reshape(1, rows), voxels)
    got = exchange(send)

    split = parts > 1
    outs, specs = [slots(1 if split else parts)], [VMEM]
    if split:
        outs += [
            jax.ShapeDtypeStruct((rows, width), BF16),
            jax.ShapeDtypeStruct(*qk),
            jax.ShapeDtypeStruct(*vt),
            jax.ShapeDtypeStruct((SUB, rows), F32),
            jax.ShapeDtypeStruct((SUB, rows // parts), I32),
        ]
        specs += [ANY, ANY, ANY, VMEM, VMEM]
    sends = call(
        functools.partial(open_kernel, parts=parts, split=split),
        "open",
        outs,
        [SMEM, VMEM, VMEM, VMEM, ANY, ANY, ANY, ANY],
        specs,
        scratch=[
            patch,
            patch,
            id_rows,
            slot_ids_scratch,
            pltpu.VMEM(*qk),
            pltpu.VMEM(*vt),
            *tile_scratch,
            *weight_scratch,
            pltpu.SemaphoreType.DMA((4,)),
            pltpu.SemaphoreType.DMA((3,)),
        ],
        flops=full_flops // 2,
    )(me, got, parent, norm_gains, *weights)
    gots = [exchange(sends[0])]
    if split:
        send = call(
            functools.partial(rest_kernel, parts=parts),
            "rest",
            slots(parts - 1),
            [SMEM, VMEM, VMEM, VMEM, VMEM, VMEM, VMEM, ANY, ANY, ANY, ANY],
            scratch=[
                patch,
                slot_ids_scratch,
                *tile_scratch,
                *weight_scratch[1:],
                pltpu.SemaphoreType.DMA((3,)),
            ],
            flops=full_flops // 2,
        )(me, *sends[1:], norm_gains, *weights)
        gots.append(exchange(send))

    send, label = call(
        functools.partial(second_kernel, parts=parts, chunks=len(gots), cap_groups=cap_groups),
        "second",
        [
            jax.ShapeDtypeStruct((n_dev * cap_groups, width), BF16),
            jax.ShapeDtypeStruct((SUB, n_dev * cap_groups), F32),
        ],
        [VMEM] * (len(gots) + 2) + [ANY] * 4,
        [VMEM, VMEM],
        scratch=[
            patch,
            patch,
            id_rows,
            pltpu.VMEM(*qk),
            pltpu.VMEM(*vt),
            *tile_scratch,
            *weight_scratch,
            pltpu.SemaphoreType.DMA((4,)),
        ],
        flops=full_flops,
    )(*gots, parent, norm_gains, *weights)
    got = exchange(send.reshape(n_dev, cap_groups, width)).reshape(n_dev * cap_groups, width)
    return call(
        pool_kernel,
        "pool",
        jax.ShapeDtypeStruct((groups, width), F32),
        [VMEM, VMEM],
    )(label, got)


def solution(mesh):
    placed = (P("vox", None), P("vox"), P("vox"), P("vox"), P(), P(), P(), P(), P())
    return jax.shard_map(
        shards, mesh=mesh, in_specs=placed, out_specs=P("vox", None), check_vma=False
    )
```

```python
import functools

import jax
import jax.numpy as jnp
from jax import lax
from jax.experimental import pallas as pl
from jax.experimental.pallas import tpu as pltpu
from jax.sharding import PartitionSpec as P

HEADS = 8
LANES = 128
SUB = 8
GROUP = 8
TILE = 256
PART = 16
LABEL_ROW = 7
F32 = jnp.float32
BF16 = jnp.bfloat16
I32 = jnp.int32
LOG2E = 1.4426950408889634
GELU_C = 0.7978845608028654
ONES = 16
NT = (((1,), (1,)), ((), ()))


def dot(a, b, dims=(((1,), (0,)), ((), ()))):
    return lax.dot_general(a, b, dims, preferred_element_type=F32)


def iota(shape, axis):
    return lax.broadcasted_iota(I32, shape, axis)


def one_hot(mask):
    return mask.astype(F32).astype(BF16)


def log2(value):
    bits = value.bit_length() - 1
    assert 1 << bits == value
    return bits


def tile_at(t):
    return pl.ds(t * TILE if isinstance(t, int) else pl.multiple_of(t * TILE, TILE), TILE)


def lane_cuts(size):
    return range(0, size, LANES)


def rank_rows(dest, n_dev):
    tri = (iota((LANES, LANES), 0) <= iota((LANES, LANES), 1)).astype(F32)
    tri = jnp.concatenate([tri, jnp.ones((LANES, LANES), F32)], axis=1).astype(BF16)
    dev = iota((n_dev, LANES), 0)
    seen = jnp.zeros((n_dev, LANES), F32)
    chunks = []
    for at in lane_cuts(dest.shape[1]):
        hot = (dest[:, at : at + LANES] == dev).astype(F32)
        both = dot(hot.astype(BF16), tri)
        chunks.append((hot, both[:, :LANES] + seen))
        seen = seen + both[:, LANES:]
    return chunks, seen


def pick(hot, table):
    return jnp.sum(hot * table, axis=0, keepdims=True)


def part_starts(counts, parts):
    n_dev = counts.shape[0]
    below = one_hot(iota((n_dev, n_dev), 1) < iota((n_dev, n_dev), 0))
    return dot(below, counts.astype(BF16)) * (1.0 / parts)


def sort_places(dest, n_dev, rows, parts):
    chunks, counts = rank_rows(dest, n_dev)
    starts = part_starts(counts, parts)
    part_rows = rows // parts
    cap = parts * PART
    places = []
    for hot, run in chunks:
        order = pick(hot, run - 1).astype(I32)
        count = pick(hot, counts).astype(I32)
        start = pick(hot, starts).astype(I32)
        full = count == cap
        part = jnp.where(full, order >> log2(PART), order >> log2(PART // 2))
        inside = order - part * jnp.where(full, PART, PART // 2)
        places.append(jnp.where(count > 0, part * part_rows + start + inside, -1))
    return jnp.concatenate(places, axis=1), counts, starts


def part_slots(counts, starts, part_rows, parts):
    n_dev = counts.shape[0]
    share = counts * (1.0 / parts)
    dev = iota((n_dev, LANES), 0).astype(F32) * PART
    slots = []
    for at in lane_cuts(part_rows):
        k = (iota((n_dev, LANES), 1) + at).astype(F32)
        inside = ((k >= starts) & (k < starts + share)).astype(F32)
        slots.append(pick(inside, dev + k - starts))
    return jnp.concatenate(slots, axis=1).astype(I32)


def group_slots(parent, n_dev, stride):
    chunks, _ = rank_rows(parent >> log2(parent.shape[1]), n_dev)
    dev = iota((n_dev, LANES), 0).astype(F32) * stride
    return jnp.concatenate([pick(hot, run - 1 + dev) for hot, run in chunks], axis=1).astype(I32)


def emit_rows(slot_row, rows, group, out_ref):
    lanes_of = rows.shape[1] // LANES
    for t in range(out_ref.shape[0] * PART // TILE):
        hot = one_hot(slot_row - t * TILE == iota((TILE, slot_row.shape[1]), 0))
        placed = dot(hot, rows).astype(BF16)
        for d in range(TILE // PART):
            for c in range(lanes_of):
                at = (group * lanes_of + c) * PART
                out_ref[t * (TILE // PART) + d, at : at + PART, :] = placed[
                    d * PART : (d + 1) * PART, c * LANES : (c + 1) * LANES
                ]


def place_ids(slot_row, meta, ids_ref):
    for t in range(ids_ref.shape[1] // TILE):
        hot = one_hot(slot_row - t * TILE == iota((TILE, slot_row.shape[1]), 0))
        ids_ref[:, tile_at(t)] += dot(meta, hot, NT)


def emit_ids(me, out_ref, ids_ref):
    per_tile = LANES // PART
    mine = lax.rem(me, per_tile)
    owned = iota((SUB, LANES), 1) // PART == mine
    at = out_ref.shape[1] - SUB
    for dev in range(out_ref.shape[0]):
        cut = dev // per_tile * LANES
        turn = lax.rem(mine + (per_tile - dev % per_tile), per_tile) * PART
        part = pltpu.roll(ids_ref[:, cut : cut + LANES], turn, 1)
        out_ref[dev, at:, :] = jnp.where(owned, part, 0.0).astype(BF16)


def slot_ids(got_ref):
    n_dev, depth, _ = got_ref.shape
    per_tile = LANES // PART
    tiles = []
    for first in range(0, n_dev, per_tile):
        total = got_ref[first, depth - SUB :, :].astype(F32)
        for j in range(1, per_tile):
            total = total + got_ref[first + j, depth - SUB :, :].astype(F32)
        tiles.append(total)
    return jnp.concatenate(tiles, axis=1)


def slot_rows(got_ref, group, lanes_of, first=0, count=None):
    n_dev = got_ref.shape[0]
    count = lanes_of if count is None else count
    return jnp.concatenate(
        [
            got_ref[:, (group * lanes_of + c) * PART : (group * lanes_of + c + 1) * PART, :].reshape(
                n_dev * PART, LANES
            )
            for c in range(first, first + count)
        ],
        axis=1,
    )


def start_all(pairs, sems, first=0):
    copies = [pltpu.make_async_copy(src, dst, sems.at[first + i]) for i, (src, dst) in enumerate(pairs)]
    for copy in copies:
        copy.start()
    return copies


def wait_all(copies):
    for copy in copies:
        copy.wait()


def slot_loads(got_hbm, got_ref, sems, first=0):
    at = got_ref.shape[1] - SUB
    return start_all(
        [(got_hbm.at[:, at:, :], got_ref.at[:, at:, :]), (got_hbm.at[:, :at, :], got_ref.at[:, :at, :])], sems, first
    )


def layer_norm(stream, gain_row):
    row_mean = jnp.mean(stream, axis=-1, keepdims=True)
    centred = stream - row_mean
    row_var = jnp.mean(centred * centred, axis=-1, keepdims=True)
    return centred * lax.rsqrt(row_var + 1e-05) * gain_row


def gelu(x):
    inner = x * (x * x * (0.044715 * GELU_C) + GELU_C)
    half = 0.5 * x
    return half + half * jnp.tanh(inner)


def project_tile(t, x_ref, qk_ref, vt_ref, qkv_w, gains):
    width = x_ref.shape[1]
    head = width // HEADS
    at = tile_at(t)
    normed = layer_norm(x_ref[at, :].astype(F32), gains[0:1, :]).astype(BF16)
    qk_ref[at, :width] = (dot(normed, qkv_w[:, :width]) * (LOG2E * head**-0.5)).astype(BF16)
    qk_ref[at, width:] = dot(normed, qkv_w[:, width : 2 * width]).astype(BF16)
    values = dot(normed, qkv_w[:, 2 * width :]).T.astype(BF16)
    for h in range(HEADS):
        vt_ref[h, :head, at] = values[h * head : (h + 1) * head, :]


def fill_ones(vt_ref):
    depth = vt_ref.shape[1]
    for h in range(HEADS):
        vt_ref[h, depth - ONES :, :] = jnp.ones((ONES, vt_ref.shape[2]), BF16)


def run_tiles(low, high, x_ref, y_ref, state, weights, gains, before_mix=(), before_join=()):
    qk_ref, vt_ref, att_ref, mid_ref, sum_ref, score_ref = state
    _, out_w, up_w, down_w = weights
    rows, width = x_ref.shape
    head = width // HEADS
    pairs = width // LANES
    per_pair = LANES // head
    piece = up_w.shape[1] // pairs
    owner = iota((TILE, LANES), 1) // head
    cuts = [slice(at, at + TILE) for at in range(0, rows, TILE)]

    def masked_queries(t, pair):
        queries = qk_ref[tile_at(t), pair * LANES : (pair + 1) * LANES]
        return [jnp.where(owner == j, queries, jnp.zeros_like(queries)) for j in range(per_pair)]

    def score(own, pair, cut):
        key_rows = qk_ref[cut, width + pair * LANES : width + (pair + 1) * LANES]
        return [dot(key_rows, own[j], NT) for j in range(per_pair)]

    def keep(scores, pair, cut, tops):
        result = []
        for j in range(per_pair):
            score_ref[pair % 2, j, cut, :] = scores[j]
            top = jnp.max(scores[j].reshape(TILE // SUB, SUB, TILE), axis=0)
            result.append(top if tops is None else jnp.maximum(tops[j], top))
        return result

    def soften(pair, cut, tops):
        return [jnp.exp2(score_ref[pair % 2, j, cut, :] - tops[j]).astype(BF16) for j in range(per_pair)]

    def mix(pair, cut, probs, sums):
        result = []
        for j in range(per_pair):
            mixed = dot(vt_ref[pair * per_pair + j, :, cut], probs[j])
            result.append(mixed if sums is None else sums[j] + mixed)
        return result

    def attend_pair(pair, tops, next_tile):
        after = (pair + 1) % pairs
        own = None if next_tile is None else masked_queries(next_tile, after)
        tops = [jnp.max(top, axis=0, keepdims=True) for top in tops]
        next_tops, sums = None, None
        for cut in cuts:
            scores = None if own is None else score(own, after, cut)
            probs = soften(pair, cut, tops)
            if own is not None:
                next_tops = keep(scores, after, cut, next_tops)
            sums = mix(pair, cut, probs, sums)
        for j in range(per_pair):
            h = pair * per_pair + j
            share = 1.0 / sums[j][head : head + SUB, :]
            mixed = sums[j][:head, :].reshape(head // SUB, SUB, TILE) * share[None]
            att_ref[h * head : (h + 1) * head, :] = mixed.reshape(head, TILE)
        return next_tops

    def join(t):
        attended = att_ref[...].T.astype(BF16)
        stream = x_ref[tile_at(t), :].astype(F32) + dot(attended, out_w[...])
        sum_ref[...] = stream
        mid_ref[...] = layer_norm(stream, gains[1:2, :]).astype(BF16)

    def mlp_piece(i):
        cut = slice(i * piece, (i + 1) * piece)
        inner = gelu(dot(mid_ref[...], up_w[:, cut])).astype(BF16)
        sum_ref[...] += dot(inner, down_w[cut, :])

    def attend_tile(t, tops, after, beside):
        for i in range(pairs):
            tops = attend_pair(i, tops, t if i + 1 < pairs else after)
            if beside:
                mlp_piece(i)
        return tops

    def step(t, tops):
        join(t - 1)
        tops = attend_tile(t, tops, jnp.minimum(t + 1, high - 1), True)
        y_ref[tile_at(t - 1), :] = sum_ref[...].astype(BF16)
        return tops

    own = masked_queries(low, 0)
    tops = None
    for cut in cuts:
        tops = keep(score(own, 0, cut), 0, cut, tops)
    wait_all(before_mix)
    tops = attend_tile(low, tops, low + 1 if high > low + 1 else None, False)
    wait_all(before_join)
    if high > low + 1:
        lax.fori_loop(low + 1, high, step, tops)
    join(high - 1)
    for i in range(pairs):
        mlp_piece(i)
    y_ref[tile_at(high - 1), :] = sum_ref[...].astype(BF16)


def pack_kernel(me_ref, hil_ref, z_ref, x_hbm, out_hbm, x_ref, out_ref, ids_ref, sems, *, parts):
    rows, width = x_ref.shape
    n_dev = out_ref.shape[0]
    span = width // LANES * PART
    loads = start_all([(x_hbm, x_ref)], sems)
    saves = []
    part_rows = rows // parts
    shift = log2(rows)
    z = z_ref[...]
    pair = jnp.concatenate([(z >> shift) + 1, (z & (rows - 1)) >> log2(GROUP)], axis=0)
    meta = jnp.concatenate([pair] * (SUB // 2), axis=0).astype(F32).astype(BF16)
    places, counts, starts = sort_places(hil_ref[...] >> shift, n_dev, rows, parts)
    slot_row = part_slots(counts, starts, part_rows, parts)
    wait_all(loads)
    total = None
    for q in range(parts):
        hot = one_hot(places - q * part_rows == iota((part_rows, rows), 0))
        sorted_rows = dot(hot, x_ref[...]).astype(BF16)
        ids = dot(meta, hot, NT)
        ids = jnp.where(iota(ids.shape, 0) // 2 == q, ids, 0.0)
        total = ids if total is None else total + ids
        emit_rows(slot_row, sorted_rows, q, out_ref)
        cut = pl.ds(q * span, span)
        saves += start_all([(out_ref.at[:, cut, :], out_hbm.at[:, cut, :])], sems, 1 + q)
    ids_ref[...] = jnp.zeros_like(ids_ref)
    place_ids(slot_row, total.astype(BF16), ids_ref)
    emit_ids(me_ref[0], out_ref, ids_ref)
    cut = pl.ds(parts * span, SUB)
    saves += start_all([(out_ref.at[:, cut, :], out_hbm.at[:, cut, :])], sems, 1 + parts)
    wait_all(saves)


def label_kernel(parent_ref, ids_ref, *, n_dev):
    parent = parent_ref[...]
    low = (parent & (parent.shape[1] - 1)) + 1
    low = jnp.broadcast_to(low, (SUB, low.shape[1])).astype(F32)
    low = jnp.where(iota(low.shape, 0) == LABEL_ROW, low, 0.0).astype(BF16)
    ids_ref[...] = jnp.zeros_like(ids_ref)
    place_ids(group_slots(parent, n_dev, PART), low, ids_ref)


def open_kernel(me_ref, got_hbm, label_ref, gains_ref, *refs, parts, split):
    hbm, refs = refs[:4], refs[4:]
    if split:
        (send_ref, x_out, qk_out, vt_out, slot_out), refs = refs[:5], refs[5:]
    else:
        (send_ref,), refs = refs[:1], refs[1:]
    x_ref, y_ref, parents_ref, ids_ref = refs[:4]
    state, weights, got_ref, sems, out_sems = refs[4:10], refs[10:14], refs[14], refs[15], refs[16]
    qk_ref, vt_ref = state[:2]
    rows, width = x_ref.shape
    n_dev = got_ref.shape[0]
    part_rows = rows // parts
    lanes_of = width // LANES
    gots = slot_loads(got_hbm, got_ref, sems)
    gains = gains_ref[0]
    fill_ones(vt_ref)

    gots[0].wait()
    ids = slot_ids(got_ref)
    dest = jnp.concatenate([ids[2 * g : 2 * g + 1, :] for g in range(parts)], axis=1).astype(I32) - 1
    parents = jnp.concatenate([ids[2 * g + 1 : 2 * g + 2, :] for g in range(parts)], axis=1) + 1.0
    parents = jnp.broadcast_to(parents, (SUB, parents.shape[1])).astype(BF16)
    places, counts, starts = sort_places(dest, n_dev, rows, parts)
    slot_row = part_slots(counts, starts, part_rows, parts)

    gots[1].wait()
    loads = start_all([(src.at[0], dst) for src, dst in zip(hbm, weights)], sems, 2)

    def receive(t, carry):
        hot = one_hot(places - t * TILE == iota((TILE, places.shape[1]), 0))
        for c in range(0, lanes_of, 2):
            data = jnp.concatenate([slot_rows(got_ref, g, lanes_of, c, 2) for g in range(parts)], axis=0)
            x_ref[tile_at(t), c * LANES : (c + 2) * LANES] = dot(hot, data).astype(BF16)
        parents_ref[:, tile_at(t)] = dot(parents, hot, NT)
        return carry

    lax.fori_loop(0, rows // TILE, receive, 0)
    loads[0].wait()

    def project(t, carry):
        project_tile(t, x_ref, qk_ref, vt_ref, weights[0], gains)
        return carry

    lax.fori_loop(0, rows // TILE, project, 0)
    saves = []
    if split:
        slot_out[...] = jnp.broadcast_to(slot_row, slot_out.shape)
        saves = start_all([(x_ref, x_out), (qk_ref, qk_out), (vt_ref, vt_out)], out_sems)
    groups = 1 if split else parts
    run_tiles(0, groups * part_rows // TILE, x_ref, y_ref, state, weights, gains, (), loads[1:])

    ids_ref[...] = label_ref[...]
    meta = [parents_ref[0:1, g * part_rows : (g + 1) * part_rows] for g in range(parts)]
    meta.append(jnp.zeros((SUB - parts, part_rows), F32))
    place_ids(slot_row, jnp.concatenate(meta, axis=0).astype(BF16), ids_ref)
    for g in range(groups):
        emit_rows(slot_row, y_ref[g * part_rows : (g + 1) * part_rows, :], g, send_ref)
    emit_ids(me_ref[0], send_ref, ids_ref)
    wait_all(saves)


def rest_kernel(x_hbm, qk_hbm, vt_hbm, slot_ref, gains_ref, *refs, parts):
    hbm, send_ref, (x_ref, y_ref, qk_ref, vt_ref), refs = refs[:4], refs[4], refs[5:9], refs[9:]
    scratch, weights, sems = refs[:4], refs[4:7], refs[7]
    low = x_ref.shape[0] // parts // TILE
    state = start_all(
        [
            (qk_hbm.at[tile_at(low), :], qk_ref.at[tile_at(low), :]),
            (qk_hbm.at[: low * TILE, :], qk_ref.at[: low * TILE, :]),
            (qk_hbm.at[(low + 1) * TILE :, :], qk_ref.at[(low + 1) * TILE :, :]),
            (vt_hbm, vt_ref),
            (x_hbm, x_ref),
        ],
        sems,
    )
    loads = start_all([(src.at[0], dst) for src, dst in zip(hbm[1:], weights)], sems, len(state))
    wait_all(state[:3])
    rows = x_ref.shape[0]
    run_tiles(
        low,
        rows // TILE,
        x_ref,
        y_ref,
        (qk_ref, vt_ref, *scratch),
        (None, *weights),
        gains_ref[0],
        state[3:4],
        state[4:] + loads,
    )
    part_rows = rows // parts
    for g in range(1, parts):
        emit_rows(slot_ref[0:1, :], y_ref[g * part_rows : (g + 1) * part_rows, :], g - 1, send_ref)


def receive_part(got_ref, group, places, own, at, x_ref, parents_ref):
    own = jnp.broadcast_to(own, (SUB, own.shape[1])).astype(BF16)
    lanes_of = x_ref.shape[1] // LANES
    for t in range(at.start // TILE, at.stop // TILE):
        hot = one_hot(places + (at.start - t * TILE) == iota((TILE, places.shape[1]), 0))
        x_ref[tile_at(t), :] = dot(hot, slot_rows(got_ref, group, lanes_of)).astype(BF16)
        parents_ref[:, tile_at(t)] = dot(own, hot, NT)


def index_kernel(got_hbm, parent_ref, gains_ref, qkv_hbm, *refs, parts, split, cap_groups):
    (places_ref, own_ref, label_ref, slot_ref), refs = refs[:4], refs[4:]
    if split:
        (x_out, qk_out, vt_out, parents_out), refs = refs[:4], refs[4:]
    got_ref, qkv_w, sems = refs[:3]
    gots = slot_loads(got_hbm, got_ref, sems)
    load = start_all([(qkv_hbm.at[1], qkv_w)], sems, 2)
    n_dev = got_ref.shape[0]
    span = n_dev * PART
    gots[0].wait()
    ids = slot_ids(got_ref)
    slots = n_dev * cap_groups
    wide, slim = iota((span, slots), 0), iota((span, slots), 1)
    narrow = one_hot(wide == (slim >> log2(cap_groups)) * PART + (slim & (cap_groups - 1)))
    label_ref[...] = dot(ids.astype(BF16), narrow)
    slot_ref[...] = jnp.broadcast_to(group_slots(parent_ref[...], n_dev, cap_groups), slot_ref.shape)
    for g in range(parts):
        own = ids[g : g + 1, :]
        ranks, _ = rank_rows(jnp.where(own > 0.0, 0, -1), SUB)
        places = jnp.concatenate([pick(hot, run) for hot, run in ranks], axis=1).astype(I32) - 1
        places_ref[g : g + 1, :] = places
        own_ref[g : g + 1, :] = own
    gots[1].wait()
    wait_all(load)
    if split:
        receive_part(got_ref, 0, places_ref[0:1, :], own_ref[0:1, :], slice(0, x_out.shape[0]), x_out, parents_out)
        for t in range(x_out.shape[0] // TILE):
            project_tile(t, x_out, qk_out, vt_out, qkv_w, gains_ref[1])


def second_kernel(*refs, parts, split):
    got_hbm, places_ref, own_ref, slot_ref, gains_ref, refs = refs[0], refs[1], refs[2], refs[3], refs[4], refs[5:]
    if split:
        early_hbm, refs = refs[:4], refs[4:]
    hbm, send_ref, refs = refs[:4], refs[4], refs[5:]
    x_ref, y_ref, parents_ref = refs[:3]
    state, weights, got_ref, sems = refs[3:9], refs[9:13], refs[13], refs[14]
    rows, width = x_ref.shape
    n_dev = got_ref.shape[0]
    part_rows = rows // parts
    first = 1 if split else 0
    gots = start_all([(got_hbm, got_ref), (hbm[0].at[1], weights[0])], sems)
    early = []
    gains = gains_ref[1]
    fill_ones(state[1])
    gots[0].wait()
    if split:
        values = width // HEADS
        early = start_all(
            [
                (early_hbm[0], x_ref.at[:part_rows, :]),
                (early_hbm[1], state[0].at[:part_rows, :]),
                (early_hbm[2], state[1].at[:, :values, :part_rows]),
                (early_hbm[3], parents_ref.at[:, :part_rows]),
            ],
            sems,
            5,
        )
    for g in range(first, parts):
        at = slice(g * part_rows, (g + 1) * part_rows)
        receive_part(got_ref, g - first, places_ref[g : g + 1, :], own_ref[g : g + 1, :], at, x_ref, parents_ref)
    gots[1].wait()
    loads = start_all([(src.at[1], dst) for src, dst in zip(hbm[1:], weights[1:])], sems, 2)

    def project(t, carry):
        project_tile(t, x_ref, state[0], state[1], weights[0], gains)
        return carry

    lax.fori_loop(first * part_rows // TILE, rows // TILE, project, 0)
    wait_all(early)
    run_tiles(0, rows // TILE, x_ref, y_ref, state, weights, gains, (), loads)

    groups = rows // GROUP
    member = one_hot(parents_ref[0:1, :].astype(I32) - 1 == iota((groups, rows), 0))
    sums = dot(member, y_ref[...]).astype(BF16)
    slot = slot_ref[0:1, :]
    send_ref[...] = dot(one_hot(slot == iota((send_ref.shape[0], groups), 0)), sums).astype(BF16)


def pool_kernel(label_ref, got_ref, out_ref):
    label = label_ref[LABEL_ROW : LABEL_ROW + 1, :].astype(I32) - 1
    hot = one_hot(label == iota((out_ref.shape[0], label.shape[1]), 0))
    out_ref[...] = dot(hot, got_ref[...])


VMEM = pl.BlockSpec(memory_space=pltpu.VMEM)
SMEM = pl.BlockSpec(memory_space=pltpu.SMEM)
ANY = pl.BlockSpec(memory_space=pltpu.HBM)


def call(body, name, outs, in_specs, out_specs=VMEM, scratch=(), flops=0):
    return pl.pallas_call(
        body,
        out_shape=outs,
        in_specs=in_specs,
        out_specs=out_specs,
        scratch_shapes=list(scratch),
        compiler_params=pltpu.CompilerParams(vmem_limit_bytes=66_000_000),
        cost_estimate=pl.CostEstimate(flops=flops, bytes_accessed=flops // 300, transcendentals=0),
        name=name,
    )


def exchange(data):
    return lax.all_to_all(data, "vox", split_axis=0, concat_axis=0, tiled=True)


def shards(
    voxels, hilbert_rank, z_rank, parent_slot, qkv_weight, out_weight, up_weight, down_weight, norm_gains
):
    rows, width = voxels.shape
    n_dev = lax.axis_size("vox")
    me = lax.axis_index("vox").astype(I32).reshape(1)
    cap = 2 * max(rows // n_dev, 1)
    parts = max(cap // PART, 1)
    groups = rows // GROUP
    cap_groups = 2 * max(groups // n_dev, 1)
    lanes_of = width // LANES
    weights = (qkv_weight, out_weight, up_weight, down_weight)
    weight_scratch = [pltpu.VMEM(w.shape[1:], BF16) for w in weights]
    parent = parent_slot.reshape(1, groups)
    full_flops = 9_000_000 * rows

    split = parts > 1

    def slots(part_count, with_ids=True):
        depth = lanes_of * part_count * PART + (SUB if with_ids else 0)
        return jax.ShapeDtypeStruct((n_dev, depth, LANES), BF16)

    def made(*shape, dtype=BF16):
        return jax.ShapeDtypeStruct(shape, dtype)

    head = width // HEADS
    part_rows = rows // parts
    qk = pltpu.VMEM((rows, 2 * width), BF16)
    vt = pltpu.VMEM((HEADS, head + ONES, rows), BF16)
    tile_scratch = [
        pltpu.VMEM((width, TILE), F32),
        pltpu.VMEM((TILE, width), BF16),
        pltpu.VMEM((TILE, width), F32),
        pltpu.VMEM((2, LANES // head, rows, TILE), F32),
    ]
    patch = pltpu.VMEM((rows, width), BF16)
    id_rows = pltpu.VMEM((SUB, rows), F32)
    slot_lanes = pltpu.VMEM((SUB, n_dev * PART), F32)
    first_slots, rest_slots = slots(1 if split else parts), slots(parts - 1, False)

    send = call(
        functools.partial(pack_kernel, parts=parts),
        "pack",
        slots(parts),
        [SMEM, VMEM, VMEM, ANY],
        ANY,
        scratch=[
            patch,
            pltpu.VMEM(slots(parts).shape, BF16),
            slot_lanes,
            pltpu.SemaphoreType.DMA((parts + 2,)),
        ],
    )(me, hilbert_rank.reshape(1, rows), z_rank.reshape(1, rows), voxels)
    got = exchange(send)
    labels = call(
        functools.partial(label_kernel, n_dev=n_dev),
        "label",
        made(SUB, n_dev * PART, dtype=F32),
        [VMEM],
        flops=full_flops // 16,
    )(parent)

    outs, specs = [first_slots], [VMEM]
    if split:
        outs += [made(rows, width), made(rows, 2 * width), made(HEADS, head + ONES, rows)]
        outs += [made(SUB, part_rows, dtype=I32)]
        specs += [ANY, ANY, ANY, VMEM]
    sends = call(
        functools.partial(open_kernel, parts=parts, split=split),
        "open",
        outs,
        [SMEM, ANY, VMEM, VMEM, ANY, ANY, ANY, ANY],
        specs,
        scratch=[
            patch,
            patch,
            id_rows,
            slot_lanes,
            qk,
            vt,
            *tile_scratch,
            *weight_scratch,
            pltpu.VMEM(slots(parts).shape, BF16),
            pltpu.SemaphoreType.DMA((6,)),
            pltpu.SemaphoreType.DMA((3,)),
        ],
        flops=full_flops // 2,
    )(me, got, labels, norm_gains, *weights)
    got = exchange(sends[0])
    if split:
        send = call(
            functools.partial(rest_kernel, parts=parts),
            "rest",
            rest_slots,
            [ANY, ANY, ANY, VMEM, VMEM, ANY, ANY, ANY, ANY],
            scratch=[
                patch,
                patch,
                qk,
                vt,
                *tile_scratch,
                *weight_scratch[1:],
                pltpu.SemaphoreType.DMA((8,)),
            ],
            flops=full_flops // 2,
        )(*sends[1:], norm_gains, *weights)
        late = exchange(send)

    outs = [
        made(SUB, n_dev * PART, dtype=I32),
        made(SUB, n_dev * PART, dtype=F32),
        made(SUB, n_dev * cap_groups, dtype=F32),
        made(SUB, groups, dtype=I32),
    ]
    if split:
        outs += [made(part_rows, width), made(part_rows, 2 * width), made(HEADS, head, part_rows)]
        outs += [made(SUB, part_rows, dtype=F32)]
    places, own, label, slot, *early = call(
        functools.partial(index_kernel, parts=parts, split=split, cap_groups=cap_groups),
        "index",
        outs,
        [ANY, VMEM, VMEM, ANY],
        [VMEM] * len(outs),
        scratch=[pltpu.VMEM(first_slots.shape, BF16), weight_scratch[0], pltpu.SemaphoreType.DMA((3,))],
        flops=full_flops // 4,
    )(got, parent, norm_gains, qkv_weight)
    send = call(
        functools.partial(second_kernel, parts=parts, split=split),
        "second",
        made(n_dev * cap_groups, width),
        [ANY] + [VMEM] * 4 + [ANY] * (len(early) + 4),
        scratch=[
            patch,
            patch,
            id_rows,
            qk,
            vt,
            *tile_scratch,
            *weight_scratch,
            pltpu.VMEM((rest_slots if split else first_slots).shape, BF16),
            pltpu.SemaphoreType.DMA((9,)),
        ],
        flops=full_flops,
    )(late if split else got, places, own, slot, norm_gains, *early, *weights)
    got = exchange(send.reshape(n_dev, cap_groups, width)).reshape(n_dev * cap_groups, width)
    return call(
        pool_kernel,
        "pool",
        made(groups, width, dtype=F32),
        [VMEM, VMEM],
    )(label, got)


def solution(mesh):
    placed = (P("vox", None), P("vox"), P("vox"), P("vox"), P(), P(), P(), P(), P())
    return jax.shard_map(
        shards, mesh=mesh, in_specs=placed, out_specs=P("vox", None), check_vma=False
    )
```

```python
import functools

import jax
import jax.numpy as jnp
from jax import lax
from jax.experimental import pallas as pl
from jax.experimental.pallas import tpu as pltpu
from jax.sharding import PartitionSpec as P

HEADS = 8
LANES = 128
SUB = 8
GROUP = 8
TILE = 256
PART = 16
LABEL_ROW = 7
F32 = jnp.float32
BF16 = jnp.bfloat16
I32 = jnp.int32
LOG2E = 1.4426950408889634
GELU_C = 0.7978845608028654
ONES = 16
NT = (((1,), (1,)), ((), ()))


def dot(a, b, dims=(((1,), (0,)), ((), ()))):
    return lax.dot_general(a, b, dims, preferred_element_type=F32)


def iota(shape, axis):
    return lax.broadcasted_iota(I32, shape, axis)


def one_hot(mask):
    return mask.astype(F32).astype(BF16)


def log2(value):
    bits = value.bit_length() - 1
    assert 1 << bits == value
    return bits


def tile_at(t):
    return pl.ds(t * TILE if isinstance(t, int) else pl.multiple_of(t * TILE, TILE), TILE)


def lane_cuts(size):
    return range(0, size, LANES)


def rank_rows(dest, n_dev):
    tri = (iota((LANES, LANES), 0) <= iota((LANES, LANES), 1)).astype(F32)
    tri = jnp.concatenate([tri, jnp.ones((LANES, LANES), F32)], axis=1).astype(BF16)
    dev = iota((n_dev, LANES), 0)
    seen = jnp.zeros((n_dev, LANES), F32)
    chunks = []
    for at in lane_cuts(dest.shape[1]):
        hot = (dest[:, at : at + LANES] == dev).astype(F32)
        both = dot(hot.astype(BF16), tri)
        chunks.append((hot, both[:, :LANES] + seen))
        seen = seen + both[:, LANES:]
    return chunks, seen


def pick(hot, table):
    return jnp.sum(hot * table, axis=0, keepdims=True)


def part_starts(counts, parts):
    n_dev = counts.shape[0]
    below = one_hot(iota((n_dev, n_dev), 1) < iota((n_dev, n_dev), 0))
    return dot(below, counts.astype(BF16)) * (1.0 / parts)


def sort_places(dest, n_dev, rows, parts):
    chunks, counts = rank_rows(dest, n_dev)
    starts = part_starts(counts, parts)
    part_rows = rows // parts
    cap = parts * PART
    places = []
    for hot, run in chunks:
        order = pick(hot, run - 1).astype(I32)
        count = pick(hot, counts).astype(I32)
        start = pick(hot, starts).astype(I32)
        full = count == cap
        part = jnp.where(full, order >> log2(PART), order >> log2(PART // 2))
        inside = order - part * jnp.where(full, PART, PART // 2)
        places.append(jnp.where(count > 0, part * part_rows + start + inside, -1))
    return jnp.concatenate(places, axis=1), counts, starts


def part_slots(counts, starts, part_rows, parts):
    n_dev = counts.shape[0]
    share = counts * (1.0 / parts)
    dev = iota((n_dev, LANES), 0).astype(F32) * PART
    slots = []
    for at in lane_cuts(part_rows):
        k = (iota((n_dev, LANES), 1) + at).astype(F32)
        inside = ((k >= starts) & (k < starts + share)).astype(F32)
        slots.append(pick(inside, dev + k - starts))
    return jnp.concatenate(slots, axis=1).astype(I32)


def group_slots(parent, n_dev, stride):
    chunks, _ = rank_rows(parent >> log2(parent.shape[1]), n_dev)
    dev = iota((n_dev, LANES), 0).astype(F32) * stride
    return jnp.concatenate([pick(hot, run - 1 + dev) for hot, run in chunks], axis=1).astype(I32)


def emit_rows(slot_row, rows, group, out_ref):
    lanes_of = rows.shape[1] // LANES
    for t in range(out_ref.shape[0] * PART // TILE):
        hot = one_hot(slot_row - t * TILE == iota((TILE, slot_row.shape[1]), 0))
        placed = dot(hot, rows).astype(BF16)
        for d in range(TILE // PART):
            for c in range(lanes_of):
                at = (group * lanes_of + c) * PART
                out_ref[t * (TILE // PART) + d, at : at + PART, :] = placed[
                    d * PART : (d + 1) * PART, c * LANES : (c + 1) * LANES
                ]


def place_ids(slot_row, meta, ids_ref):
    for t in range(ids_ref.shape[1] // TILE):
        hot = one_hot(slot_row - t * TILE == iota((TILE, slot_row.shape[1]), 0))
        ids_ref[:, tile_at(t)] += dot(meta, hot, NT)


def emit_ids(me, out_ref, ids_ref):
    per_tile = LANES // PART
    mine = lax.rem(me, per_tile)
    owned = iota((SUB, LANES), 1) // PART == mine
    at = out_ref.shape[1] - SUB
    for dev in range(out_ref.shape[0]):
        cut = dev // per_tile * LANES
        turn = lax.rem(mine + (per_tile - dev % per_tile), per_tile) * PART
        part = pltpu.roll(ids_ref[:, cut : cut + LANES], turn, 1)
        out_ref[dev, at:, :] = jnp.where(owned, part, 0.0).astype(BF16)


def slot_ids(got_ref):
    n_dev, depth, _ = got_ref.shape
    per_tile = LANES // PART
    tiles = []
    for first in range(0, n_dev, per_tile):
        total = got_ref[first, depth - SUB :, :].astype(F32)
        for j in range(1, per_tile):
            total = total + got_ref[first + j, depth - SUB :, :].astype(F32)
        tiles.append(total)
    return jnp.concatenate(tiles, axis=1)


def slot_rows(got_ref, group, lanes_of, first=0, count=None):
    n_dev = got_ref.shape[0]
    count = lanes_of if count is None else count
    return jnp.concatenate(
        [
            got_ref[:, (group * lanes_of + c) * PART : (group * lanes_of + c + 1) * PART, :].reshape(
                n_dev * PART, LANES
            )
            for c in range(first, first + count)
        ],
        axis=1,
    )


def start_all(pairs, sems, first=0):
    copies = [pltpu.make_async_copy(src, dst, sems.at[first + i]) for i, (src, dst) in enumerate(pairs)]
    for copy in copies:
        copy.start()
    return copies


def wait_all(copies):
    for copy in copies:
        copy.wait()


def slot_loads(got_hbm, got_ref, sems, first=0):
    at = got_ref.shape[1] - SUB
    return start_all(
        [(got_hbm.at[:, at:, :], got_ref.at[:, at:, :]), (got_hbm.at[:, :at, :], got_ref.at[:, :at, :])], sems, first
    )


def layer_norm(stream, gain_row):
    row_mean = jnp.mean(stream, axis=-1, keepdims=True)
    centred = stream - row_mean
    row_var = jnp.mean(centred * centred, axis=-1, keepdims=True)
    return centred * lax.rsqrt(row_var + 1e-05) * gain_row


def gelu(x):
    inner = x * (x * x * (0.044715 * GELU_C) + GELU_C)
    half = 0.5 * x
    return half + half * jnp.tanh(inner)


def project_tile(t, x_ref, qk_ref, vt_ref, qkv_w, gains):
    width = x_ref.shape[1]
    head = width // HEADS
    at = tile_at(t)
    normed = layer_norm(x_ref[at, :].astype(F32), gains[0:1, :]).astype(BF16)
    qk_ref[at, :width] = (dot(normed, qkv_w[:, :width]) * (LOG2E * head**-0.5)).astype(BF16)
    qk_ref[at, width:] = dot(normed, qkv_w[:, width : 2 * width]).astype(BF16)
    values = dot(normed, qkv_w[:, 2 * width :]).T.astype(BF16)
    for h in range(HEADS):
        vt_ref[h, :head, at] = values[h * head : (h + 1) * head, :]


def fill_ones(vt_ref):
    depth = vt_ref.shape[1]
    for h in range(HEADS):
        vt_ref[h, depth - ONES :, :] = jnp.ones((ONES, vt_ref.shape[2]), BF16)


def run_tiles(low, high, x_ref, y_ref, state, weights, gains, before_mix=(), before_join=()):
    qk_ref, vt_ref, att_ref, mid_ref, sum_ref, score_ref = state
    _, out_w, up_w, down_w = weights
    rows, width = x_ref.shape
    head = width // HEADS
    pairs = width // LANES
    per_pair = LANES // head
    piece = up_w.shape[1] // pairs
    owner = iota((TILE, LANES), 1) // head
    cuts = [slice(at, at + TILE) for at in range(0, rows, TILE)]
    alone = high == low + 1

    def masked_queries(t, pair):
        queries = qk_ref[tile_at(t), pair * LANES : (pair + 1) * LANES]
        return [jnp.where(owner == j, queries, jnp.zeros_like(queries)) for j in range(per_pair)]

    def score(own, pair, cut):
        key_rows = qk_ref[cut, width + pair * LANES : width + (pair + 1) * LANES]
        return [dot(key_rows, own[j], NT) for j in range(per_pair)]

    def keep(scores, pair, cut, tops):
        result = []
        for j in range(per_pair):
            score_ref[pair % 2, j, cut, :] = scores[j]
            top = jnp.max(scores[j].reshape(TILE // SUB, SUB, TILE), axis=0)
            result.append(top if tops is None else jnp.maximum(tops[j], top))
        return result

    def soften(pair, cut, tops):
        return [jnp.exp2(score_ref[pair % 2, j, cut, :] - tops[j]).astype(BF16) for j in range(per_pair)]

    def mix(pair, cut, probs, sums):
        result = []
        for j in range(per_pair):
            mixed = dot(vt_ref[pair * per_pair + j, :, cut], probs[j])
            result.append(mixed if sums is None else sums[j] + mixed)
        return result

    def attend_pair(pair, tops, next_tile):
        after = (pair + 1) % pairs
        own = None if next_tile is None else masked_queries(next_tile, after)
        tops = [jnp.max(top, axis=0, keepdims=True) for top in tops]
        next_tops, sums, probs = None, None, []
        for cut in cuts:
            scores = None if own is None or alone else score(own, after, cut)
            probs.append(soften(pair, cut, tops))
            if own is not None:
                scores = score(own, after, cut) if alone else scores
                next_tops = keep(scores, after, cut, next_tops)
            if not alone:
                sums = mix(pair, cut, probs[-1], sums)
        if alone:
            probs = [jnp.concatenate([p[j] for p in probs], axis=0) for j in range(per_pair)]
            sums = mix(pair, slice(None), probs, None)
        for j in range(per_pair):
            h = pair * per_pair + j
            share = 1.0 / sums[j][head : head + SUB, :]
            mixed = sums[j][:head, :].reshape(head // SUB, SUB, TILE) * share[None]
            att_ref[h * head : (h + 1) * head, :] = mixed.reshape(head, TILE)
        return next_tops

    def join(t):
        attended = att_ref[...].T.astype(BF16)
        stream = x_ref[tile_at(t), :].astype(F32) + dot(attended, out_w[...])
        sum_ref[...] = stream
        mid_ref[...] = layer_norm(stream, gains[1:2, :]).astype(BF16)

    def mlp_piece(i):
        cut = slice(i * piece, (i + 1) * piece)
        inner = gelu(dot(mid_ref[...], up_w[:, cut])).astype(BF16)
        sum_ref[...] += dot(inner, down_w[cut, :])

    def attend_tile(t, tops, after, beside):
        for i in range(pairs):
            tops = attend_pair(i, tops, t if i + 1 < pairs else after)
            if beside:
                mlp_piece(i)
        return tops

    def step(t, tops):
        join(t - 1)
        tops = attend_tile(t, tops, jnp.minimum(t + 1, high - 1), True)
        y_ref[tile_at(t - 1), :] = sum_ref[...].astype(BF16)
        return tops

    own = masked_queries(low, 0)
    tops = None
    for cut in cuts:
        tops = keep(score(own, 0, cut), 0, cut, tops)
    wait_all(before_mix)
    tops = attend_tile(low, tops, low + 1 if high > low + 1 else None, False)
    wait_all(before_join)
    if high > low + 1:
        lax.fori_loop(low + 1, high, step, tops)
    join(high - 1)
    for i in range(pairs):
        mlp_piece(i)
    y_ref[tile_at(high - 1), :] = sum_ref[...].astype(BF16)


def pack_kernel(me_ref, hil_ref, z_ref, x_hbm, out_hbm, x_ref, out_ref, ids_ref, sems, *, parts):
    rows, width = x_ref.shape
    n_dev = out_ref.shape[0]
    span = width // LANES * PART
    loads = start_all([(x_hbm, x_ref)], sems)
    saves = []
    part_rows = rows // parts
    shift = log2(rows)
    z = z_ref[...]
    pair = jnp.concatenate([(z >> shift) + 1, (z & (rows - 1)) >> log2(GROUP)], axis=0)
    meta = jnp.concatenate([pair] * (SUB // 2), axis=0).astype(F32).astype(BF16)
    places, counts, starts = sort_places(hil_ref[...] >> shift, n_dev, rows, parts)
    slot_row = part_slots(counts, starts, part_rows, parts)
    wait_all(loads)
    total = None
    for q in range(parts):
        hot = one_hot(places - q * part_rows == iota((part_rows, rows), 0))
        sorted_rows = dot(hot, x_ref[...]).astype(BF16)
        ids = dot(meta, hot, NT)
        ids = jnp.where(iota(ids.shape, 0) // 2 == q, ids, 0.0)
        total = ids if total is None else total + ids
        emit_rows(slot_row, sorted_rows, q, out_ref)
        cut = pl.ds(q * span, span)
        saves += start_all([(out_ref.at[:, cut, :], out_hbm.at[:, cut, :])], sems, 1 + q)
    ids_ref[...] = jnp.zeros_like(ids_ref)
    place_ids(slot_row, total.astype(BF16), ids_ref)
    emit_ids(me_ref[0], out_ref, ids_ref)
    cut = pl.ds(parts * span, SUB)
    saves += start_all([(out_ref.at[:, cut, :], out_hbm.at[:, cut, :])], sems, 1 + parts)
    wait_all(saves)


def label_kernel(parent_ref, ids_ref, *, n_dev):
    parent = parent_ref[...]
    low = (parent & (parent.shape[1] - 1)) + 1
    low = jnp.broadcast_to(low, (SUB, low.shape[1])).astype(F32)
    low = jnp.where(iota(low.shape, 0) == LABEL_ROW, low, 0.0).astype(BF16)
    ids_ref[...] = jnp.zeros_like(ids_ref)
    place_ids(group_slots(parent, n_dev, PART), low, ids_ref)


def open_kernel(me_ref, got_hbm, label_ref, gains_ref, *refs, parts, split):
    hbm, refs = refs[:4], refs[4:]
    if split:
        (send_ref, x_out, qk_out, vt_out, slot_out), refs = refs[:5], refs[5:]
    else:
        (send_ref,), refs = refs[:1], refs[1:]
    x_ref, y_ref, parents_ref, ids_ref = refs[:4]
    state, weights, got_ref, sems, out_sems = refs[4:10], refs[10:14], refs[14], refs[15], refs[16]
    qk_ref, vt_ref = state[:2]
    rows, width = x_ref.shape
    n_dev = got_ref.shape[0]
    part_rows = rows // parts
    lanes_of = width // LANES
    gots = slot_loads(got_hbm, got_ref, sems)
    gains = gains_ref[0]
    fill_ones(vt_ref)

    gots[0].wait()
    ids = slot_ids(got_ref)
    packs = []
    for g in range(parts):
        both = ids[2 * g : 2 * g + 2, :] + iota((2, ids.shape[1]), 0).astype(F32)
        packs.append((pack_places(both[0:1, :]), both))
    gots[1].wait()
    loads = start_all([(src.at[0], dst) for src, dst in zip(hbm, weights)], sems, 2)
    for g, (places, both) in enumerate(packs):
        both = jnp.concatenate([both] * (SUB // 2), axis=0)
        receive_part(got_ref, g, places, both, slice(g * part_rows, (g + 1) * part_rows), y_ref, parents_ref)
    dest = parents_ref[0:1, :].astype(I32) - 1
    parents = jnp.broadcast_to(parents_ref[1:2, :], parents_ref.shape).astype(BF16)
    places, counts, starts = sort_places(dest, n_dev, rows, parts)
    slot_row = part_slots(counts, starts, part_rows, parts)

    def receive(t, carry):
        hot = one_hot(places - t * TILE == iota((TILE, places.shape[1]), 0))
        x_ref[tile_at(t), :] = dot(hot, y_ref[...]).astype(BF16)
        parents_ref[:, tile_at(t)] = dot(parents, hot, NT)
        return carry

    lax.fori_loop(0, rows // TILE, receive, 0)
    loads[0].wait()

    def project(t, carry):
        project_tile(t, x_ref, qk_ref, vt_ref, weights[0], gains)
        return carry

    lax.fori_loop(0, rows // TILE, project, 0)
    saves = []
    if split:
        slot_out[...] = jnp.broadcast_to(slot_row, slot_out.shape)
        saves = start_all([(x_ref, x_out), (qk_ref, qk_out), (vt_ref, vt_out)], out_sems)
    groups = 1 if split else parts
    run_tiles(0, groups * part_rows // TILE, x_ref, y_ref, state, weights, gains, (), loads[1:])

    ids_ref[...] = label_ref[...]
    meta = [parents_ref[0:1, g * part_rows : (g + 1) * part_rows] for g in range(parts)]
    meta.append(jnp.zeros((SUB - parts, part_rows), F32))
    place_ids(slot_row, jnp.concatenate(meta, axis=0).astype(BF16), ids_ref)
    for g in range(groups):
        emit_rows(slot_row, y_ref[g * part_rows : (g + 1) * part_rows, :], g, send_ref)
    emit_ids(me_ref[0], send_ref, ids_ref)
    wait_all(saves)


def rest_kernel(x_hbm, qk_hbm, vt_hbm, slot_ref, gains_ref, *refs, parts):
    hbm, send_ref, (x_ref, y_ref, qk_ref, vt_ref), refs = refs[:4], refs[4], refs[5:9], refs[9:]
    scratch, weights, sems = refs[:4], refs[4:7], refs[7]
    low = x_ref.shape[0] // parts // TILE
    state = start_all(
        [
            (qk_hbm.at[tile_at(low), :], qk_ref.at[tile_at(low), :]),
            (qk_hbm.at[: low * TILE, :], qk_ref.at[: low * TILE, :]),
            (qk_hbm.at[(low + 1) * TILE :, :], qk_ref.at[(low + 1) * TILE :, :]),
            (vt_hbm, vt_ref),
            (x_hbm, x_ref),
        ],
        sems,
    )
    loads = start_all([(src.at[0], dst) for src, dst in zip(hbm[1:], weights)], sems, len(state))
    wait_all(state[:3])
    rows = x_ref.shape[0]
    run_tiles(
        low,
        rows // TILE,
        x_ref,
        y_ref,
        (qk_ref, vt_ref, *scratch),
        (None, *weights),
        gains_ref[0],
        state[3:4],
        state[4:] + loads,
    )
    part_rows = rows // parts
    for g in range(1, parts):
        emit_rows(slot_ref[0:1, :], y_ref[g * part_rows : (g + 1) * part_rows, :], g - 1, send_ref)


def pack_places(own):
    ranks, _ = rank_rows(jnp.where(own > 0.0, 0, -1), SUB)
    return jnp.concatenate([pick(hot, run) for hot, run in ranks], axis=1).astype(I32) - 1


def receive_part(got_ref, group, places, own, at, x_ref, parents_ref):
    own = jnp.broadcast_to(own, (SUB, own.shape[1])).astype(BF16)
    lanes_of = x_ref.shape[1] // LANES
    for t in range(at.start // TILE, at.stop // TILE):
        hot = one_hot(places + (at.start - t * TILE) == iota((TILE, places.shape[1]), 0))
        x_ref[tile_at(t), :] = dot(hot, slot_rows(got_ref, group, lanes_of)).astype(BF16)
        parents_ref[:, tile_at(t)] = dot(own, hot, NT)


def index_kernel(got_hbm, parent_ref, gains_ref, qkv_hbm, *refs, parts, split, cap_groups):
    (places_ref, own_ref, label_ref, slot_ref), refs = refs[:4], refs[4:]
    if split:
        (x_out, qk_out, vt_out, parents_out), refs = refs[:4], refs[4:]
    got_ref, qkv_w, sems = refs[:3]
    gots = slot_loads(got_hbm, got_ref, sems)
    load = start_all([(qkv_hbm.at[1], qkv_w)], sems, 2)
    n_dev = got_ref.shape[0]
    span = n_dev * PART
    gots[0].wait()
    ids = slot_ids(got_ref)
    slots = n_dev * cap_groups
    wide, slim = iota((span, slots), 0), iota((span, slots), 1)
    narrow = one_hot(wide == (slim >> log2(cap_groups)) * PART + (slim & (cap_groups - 1)))
    label_ref[...] = dot(ids.astype(BF16), narrow)
    slot_ref[...] = jnp.broadcast_to(group_slots(parent_ref[...], n_dev, cap_groups), slot_ref.shape)
    for g in range(parts):
        own = ids[g : g + 1, :]
        places_ref[g : g + 1, :] = pack_places(own)
        own_ref[g : g + 1, :] = own
    gots[1].wait()
    wait_all(load)
    if split:
        receive_part(got_ref, 0, places_ref[0:1, :], own_ref[0:1, :], slice(0, x_out.shape[0]), x_out, parents_out)
        for t in range(x_out.shape[0] // TILE):
            project_tile(t, x_out, qk_out, vt_out, qkv_w, gains_ref[1])


def second_kernel(*refs, parts, split):
    got_hbm, places_ref, own_ref, slot_ref, gains_ref, refs = refs[0], refs[1], refs[2], refs[3], refs[4], refs[5:]
    if split:
        early_hbm, refs = refs[:4], refs[4:]
    hbm, send_ref, refs = refs[:4], refs[4], refs[5:]
    x_ref, y_ref, parents_ref = refs[:3]
    state, weights, got_ref, sems = refs[3:9], refs[9:13], refs[13], refs[14]
    rows, width = x_ref.shape
    n_dev = got_ref.shape[0]
    part_rows = rows // parts
    first = 1 if split else 0
    gots = start_all([(got_hbm, got_ref), (hbm[0].at[1], weights[0])], sems)
    early = []
    gains = gains_ref[1]
    fill_ones(state[1])
    gots[0].wait()
    if split:
        values = width // HEADS
        early = start_all(
            [
                (early_hbm[0], x_ref.at[:part_rows, :]),
                (early_hbm[1], state[0].at[:part_rows, :]),
                (early_hbm[2], state[1].at[:, :values, :part_rows]),
                (early_hbm[3], parents_ref.at[:, :part_rows]),
            ],
            sems,
            5,
        )
    for g in range(first, parts):
        at = slice(g * part_rows, (g + 1) * part_rows)
        receive_part(got_ref, g - first, places_ref[g : g + 1, :], own_ref[g : g + 1, :], at, x_ref, parents_ref)
    gots[1].wait()
    loads = start_all([(src.at[1], dst) for src, dst in zip(hbm[1:], weights[1:])], sems, 2)

    def project(t, carry):
        project_tile(t, x_ref, state[0], state[1], weights[0], gains)
        return carry

    lax.fori_loop(first * part_rows // TILE, rows // TILE, project, 0)
    wait_all(early)
    run_tiles(0, rows // TILE, x_ref, y_ref, state, weights, gains, (), loads)

    groups = rows // GROUP
    member = one_hot(parents_ref[0:1, :].astype(I32) - 1 == iota((groups, rows), 0))
    sums = dot(member, y_ref[...]).astype(BF16)
    slot = slot_ref[0:1, :]
    send_ref[...] = dot(one_hot(slot == iota((send_ref.shape[0], groups), 0)), sums).astype(BF16)


def pool_kernel(label_ref, got_ref, out_ref):
    label = label_ref[LABEL_ROW : LABEL_ROW + 1, :].astype(I32) - 1
    hot = one_hot(label == iota((out_ref.shape[0], label.shape[1]), 0))
    out_ref[...] = dot(hot, got_ref[...])


VMEM = pl.BlockSpec(memory_space=pltpu.VMEM)
SMEM = pl.BlockSpec(memory_space=pltpu.SMEM)
ANY = pl.BlockSpec(memory_space=pltpu.HBM)


def call(body, name, outs, in_specs, out_specs=VMEM, scratch=(), flops=0):
    return pl.pallas_call(
        body,
        out_shape=outs,
        in_specs=in_specs,
        out_specs=out_specs,
        scratch_shapes=list(scratch),
        compiler_params=pltpu.CompilerParams(vmem_limit_bytes=66_000_000),
        cost_estimate=pl.CostEstimate(flops=flops, bytes_accessed=flops // 300, transcendentals=0),
        name=name,
    )


def exchange(data):
    return lax.all_to_all(data, "vox", split_axis=0, concat_axis=0, tiled=True)


def shards(
    voxels, hilbert_rank, z_rank, parent_slot, qkv_weight, out_weight, up_weight, down_weight, norm_gains
):
    rows, width = voxels.shape
    n_dev = lax.axis_size("vox")
    me = lax.axis_index("vox").astype(I32).reshape(1)
    cap = 2 * max(rows // n_dev, 1)
    parts = max(cap // PART, 1)
    groups = rows // GROUP
    cap_groups = 2 * max(groups // n_dev, 1)
    lanes_of = width // LANES
    weights = (qkv_weight, out_weight, up_weight, down_weight)
    weight_scratch = [pltpu.VMEM(w.shape[1:], BF16) for w in weights]
    parent = parent_slot.reshape(1, groups)
    full_flops = 9_000_000 * rows

    split = parts > 1

    def slots(part_count, with_ids=True):
        depth = lanes_of * part_count * PART + (SUB if with_ids else 0)
        return jax.ShapeDtypeStruct((n_dev, depth, LANES), BF16)

    def made(*shape, dtype=BF16):
        return jax.ShapeDtypeStruct(shape, dtype)

    head = width // HEADS
    part_rows = rows // parts
    qk = pltpu.VMEM((rows, 2 * width), BF16)
    vt = pltpu.VMEM((HEADS, head + ONES, rows), BF16)
    tile_scratch = [
        pltpu.VMEM((width, TILE), F32),
        pltpu.VMEM((TILE, width), BF16),
        pltpu.VMEM((TILE, width), F32),
        pltpu.VMEM((2, LANES // head, rows, TILE), F32),
    ]
    patch = pltpu.VMEM((rows, width), BF16)
    id_rows = pltpu.VMEM((SUB, rows), F32)
    slot_lanes = pltpu.VMEM((SUB, n_dev * PART), F32)
    first_slots, rest_slots = slots(1 if split else parts), slots(parts - 1, False)

    send = call(
        functools.partial(pack_kernel, parts=parts),
        "pack",
        slots(parts),
        [SMEM, VMEM, VMEM, ANY],
        ANY,
        scratch=[
            patch,
            pltpu.VMEM(slots(parts).shape, BF16),
            slot_lanes,
            pltpu.SemaphoreType.DMA((parts + 2,)),
        ],
    )(me, hilbert_rank.reshape(1, rows), z_rank.reshape(1, rows), voxels)
    got = exchange(send)
    labels = call(
        functools.partial(label_kernel, n_dev=n_dev),
        "label",
        made(SUB, n_dev * PART, dtype=F32),
        [VMEM],
        flops=full_flops // 16,
    )(parent)

    outs, specs = [first_slots], [VMEM]
    if split:
        outs += [made(rows, width), made(rows, 2 * width), made(HEADS, head + ONES, rows)]
        outs += [made(SUB, part_rows, dtype=I32)]
        specs += [ANY, ANY, ANY, VMEM]
    sends = call(
        functools.partial(open_kernel, parts=parts, split=split),
        "open",
        outs,
        [SMEM, ANY, VMEM, VMEM, ANY, ANY, ANY, ANY],
        specs,
        scratch=[
            patch,
            patch,
            id_rows,
            slot_lanes,
            qk,
            vt,
            *tile_scratch,
            *weight_scratch,
            pltpu.VMEM(slots(parts).shape, BF16),
            pltpu.SemaphoreType.DMA((6,)),
            pltpu.SemaphoreType.DMA((3,)),
        ],
        flops=full_flops // 2,
    )(me, got, labels, norm_gains, *weights)
    got = exchange(sends[0])
    if split:
        send = call(
            functools.partial(rest_kernel, parts=parts),
            "rest",
            rest_slots,
            [ANY, ANY, ANY, VMEM, VMEM, ANY, ANY, ANY, ANY],
            scratch=[
                patch,
                patch,
                qk,
                vt,
                *tile_scratch,
                *weight_scratch[1:],
                pltpu.SemaphoreType.DMA((8,)),
            ],
            flops=full_flops // 2,
        )(*sends[1:], norm_gains, *weights)
        late = exchange(send)

    outs = [
        made(SUB, n_dev * PART, dtype=I32),
        made(SUB, n_dev * PART, dtype=F32),
        made(SUB, n_dev * cap_groups, dtype=F32),
        made(SUB, groups, dtype=I32),
    ]
    if split:
        outs += [made(part_rows, width), made(part_rows, 2 * width), made(HEADS, head, part_rows)]
        outs += [made(SUB, part_rows, dtype=F32)]
    places, own, label, slot, *early = call(
        functools.partial(index_kernel, parts=parts, split=split, cap_groups=cap_groups),
        "index",
        outs,
        [ANY, VMEM, VMEM, ANY],
        [VMEM] * len(outs),
        scratch=[pltpu.VMEM(first_slots.shape, BF16), weight_scratch[0], pltpu.SemaphoreType.DMA((3,))],
        flops=full_flops // 4,
    )(got, parent, norm_gains, qkv_weight)
    send = call(
        functools.partial(second_kernel, parts=parts, split=split),
        "second",
        made(n_dev * cap_groups, width),
        [ANY] + [VMEM] * 4 + [ANY] * (len(early) + 4),
        scratch=[
            patch,
            patch,
            id_rows,
            qk,
            vt,
            *tile_scratch,
            *weight_scratch,
            pltpu.VMEM((rest_slots if split else first_slots).shape, BF16),
            pltpu.SemaphoreType.DMA((9,)),
        ],
        flops=full_flops,
    )(late if split else got, places, own, slot, norm_gains, *early, *weights)
    got = exchange(send.reshape(n_dev, cap_groups, width)).reshape(n_dev * cap_groups, width)
    return call(
        pool_kernel,
        "pool",
        made(groups, width, dtype=F32),
        [VMEM, VMEM],
    )(label, got)


def solution(mesh):
    placed = (P("vox", None), P("vox"), P("vox"), P("vox"), P(), P(), P(), P(), P())
    return jax.shard_map(
        shards, mesh=mesh, in_specs=placed, out_specs=P("vox", None), check_vma=False
    )
```
